128 devices in a mesh: ctx: 16 (over y, z_lo, core), head: 8 (over x, z_hi).
Axes of the slice: x: 4, y: 4, z: 4 (z_hi: 2, z_lo: 2; z = z_hi * 2 + z_lo), core: 2. Of those that a mesh axis runs over, the one named last changes fastest.
Arguments:
- queries: bfloat16 [16384, 4096], P('ctx', 'head'), may hold values from -9 to 9
- rotated_key_rows: bfloat16 [16384, 1024], P(('ctx', 'head')), may hold values from -4 to 4
- value_row_matrix: bfloat16 [16384, 1024], P(('ctx', 'head')), may hold values from -5 to 5
- output_gradient: bfloat16 [16384, 4096], P('ctx', 'head'), may hold values from -5 to 5
- vertical: int32 [8, 4], P('head'), may hold values from 0 to 127, as said below
- slash_band_width: int32 [32], P('head'), may hold values from 128 to 512, as said below
Outputs:
- attention: bfloat16 [16384, 4096], P('ctx', 'head')
- grad_queries: bfloat16 [16384, 4096], P('ctx', 'head')
- key_gradient_rows: bfloat16 [16384, 1024], P(('ctx', 'head'))
- value_gradient_rows: bfloat16 [16384, 1024], P(('ctx', 'head'))
The draws below stay inside these ranges and needn't reach their ends.
Inputs may be any that keep to these rules, and one draw needn't show every extreme that they name: `vertical`: the 4 blocks of one KV head are distinct. `slash_band_width`: some query head has a band of exactly 512 keys.
All inputs are finite; a program needn't handle non-finite values.
Results may differ from the reference program's by a relative error of at most 0.03.
Values may be sent and summed in bfloat16 or wider, within the bound.
A program may use at most 64 MiB of HBM per device.

```python
import math
import jax
import jax.numpy as jnp
from jax import lax

QUERY_HEADS = 32
KEY_VALUE_HEADS = 8
HEAD_SIZE = 128
SLASH_KEYS_MAX = 512
BLOCK_POSITIONS = 128
VERTICAL_BLOCKS = 4
SEQUENCE_LENGTH = 16384
NBLK = 128


def draw_rotated_key_rows(key, part):
    unmasked_scores = jnp.clip(jax.random.normal(jax.random.fold_in(key, 42), (SEQUENCE_LENGTH, KEY_VALUE_HEADS * HEAD_SIZE), jnp.float32), -4.0, 4.0)
    return unmasked_scores.astype(jnp.bfloat16)


def draw_queries(key, part):
    unmasked_scores = jnp.clip(jax.random.normal(jax.random.fold_in(key, 43), (SEQUENCE_LENGTH, QUERY_HEADS * HEAD_SIZE), jnp.float32), -4.0, 4.0)
    return unmasked_scores.astype(jnp.bfloat16)


def draw_vertical(key, part):
    chosen = []
    for head_index_value in range(KEY_VALUE_HEADS):
        order = jax.random.permutation(jax.random.fold_in(key, 100 + head_index_value), NBLK - 2) + 1
        chosen.append(order[:VERTICAL_BLOCKS].astype(jnp.int32))
    table = jnp.stack(chosen)
    selected_blocks = jax.random.randint(jax.random.fold_in(key, 99), (), 0, KEY_VALUE_HEADS)
    table = table.at[selected_blocks, 0].set(NBLK - 1)
    table = table.at[selected_blocks, 1].set(0)
    return table.astype(jnp.int32)


def draw_slash_band_width(key, part):
    band_width_list = jax.random.randint(jax.random.fold_in(key, 71), (QUERY_HEADS,), SLASH_KEYS_MAX // 4, SLASH_KEYS_MAX + 1)
    selected_blocks = jax.random.randint(jax.random.fold_in(key, 72), (), 0, QUERY_HEADS)
    return band_width_list.at[selected_blocks].set(SLASH_KEYS_MAX).astype(jnp.int32)


def shard_levels(key, shape, pieces, least, largest):
    def one(dim, shards_of):
        heights = jax.random.uniform(jax.random.fold_in(jax.random.fold_in(key, 6), dim), (shards_of,), jnp.float32, least / len(pieces), largest / len(pieces))
        return jnp.repeat(jnp.exp(heights), shape[dim] // shards_of).reshape((-1,) + (1,) * (len(shape) - dim - 1))

    gain = one(*pieces[0])
    for cut in pieces[1:]:
        gain = gain * one(*cut)
    return gain


def normal_values(key, extent, width, limit, pieces=(), held_as=jnp.bfloat16):
    array = jax.random.normal(key, extent, jnp.float32) * width
    if len(pieces) > 0:
        array = shard_levels(key, extent, pieces, -0.22, 0.18) * array
    return jnp.clip(array, min=-limit, max=limit).astype(held_as)


def setup_inputs(seed: int = 0) -> dict:
    seeds = jax.random.split(jax.random.key(seed), 7)
    queries = draw_queries(jax.random.fold_in(seeds[6], 71), 0)
    rotated_key_rows = draw_rotated_key_rows(jax.random.fold_in(seeds[6], 71), 0)
    value_row_matrix = normal_values(seeds[2], (SEQUENCE_LENGTH, KEY_VALUE_HEADS * HEAD_SIZE), 1.0, 5.0, ((0, 128),))
    output_gradient = normal_values(seeds[3], (SEQUENCE_LENGTH, QUERY_HEADS * HEAD_SIZE), 1.0, 5.0, ((0, 16), (1, 8)))
    vertical = draw_vertical(jax.random.fold_in(seeds[6], 71), 0)
    slash_band_width = draw_slash_band_width(jax.random.fold_in(seeds[6], 71), 0)
    return dict(queries=queries, rotated_key_rows=rotated_key_rows, value_row_matrix=value_row_matrix, output_gradient=output_gradient, vertical=vertical, slash_band_width=slash_band_width)


NEG_FILL = -1e+30

def attention_mask(query_pos, band_pos, vertical_positions, band_width_list):
    gap = query_pos[:, None] - band_pos[None, :]
    band_ok = (gap >= 0) & (band_pos[None, :] >= 0)
    band_ok = band_ok[None, None] & (gap[None, None] < band_width_list[:, :, None, None])
    vert_gap = query_pos[None, :, None] - vertical_positions[:, None, :]
    vert_ok = vert_gap[:, None] >= band_width_list[:, :, None, None]
    return jnp.concatenate([band_ok, vert_ok], 3)

def reference(queries, rotated_key_rows, value_row_matrix, output_gradient, vertical, slash_band_width):
    sequence_count = queries.shape[0]
    queries_per_group = QUERY_HEADS // KEY_VALUE_HEADS
    score_scale = 1.0 / math.sqrt(HEAD_SIZE)
    key_head_split = rotated_key_rows.astype(jnp.float32).reshape(sequence_count, KEY_VALUE_HEADS, HEAD_SIZE).transpose(1, 0, 2)
    value_head_split = value_row_matrix.astype(jnp.float32).reshape(sequence_count, KEY_VALUE_HEADS, HEAD_SIZE).transpose(1, 0, 2)
    zeroed_border = jnp.zeros((KEY_VALUE_HEADS, SLASH_KEYS_MAX, HEAD_SIZE), jnp.float32)
    key_padded = jnp.concatenate([zeroed_border, key_head_split], 1)
    value_padded = jnp.concatenate([zeroed_border, value_head_split], 1)
    vertical_positions = (vertical[:, :, None] * BLOCK_POSITIONS + jnp.arange(BLOCK_POSITIONS, dtype=jnp.int32)[None, None, :]).reshape(KEY_VALUE_HEADS, VERTICAL_BLOCKS * BLOCK_POSITIONS).astype(jnp.int32)
    head_index_list = jnp.arange(KEY_VALUE_HEADS, dtype=jnp.int32)[:, None]
    vert_key = key_head_split[head_index_list, vertical_positions]
    vert_value = value_head_split[head_index_list, vertical_positions]
    band_width_list = slash_band_width.reshape(KEY_VALUE_HEADS, queries_per_group)
    block_row_span = 512 if sequence_count % 512 == 0 else sequence_count
    span = SLASH_KEYS_MAX + block_row_span

    def step(carry, block_number):
        pad_key, pad_value, acc_key, acc_value = carry
        first_row_index = (block_number * block_row_span).astype(jnp.int32)
        query_block = lax.dynamic_slice_in_dim(queries, first_row_index, block_row_span, 0).astype(jnp.float32).reshape(block_row_span, KEY_VALUE_HEADS, queries_per_group, HEAD_SIZE)
        block_gradient = lax.dynamic_slice_in_dim(output_gradient, first_row_index, block_row_span, 0).astype(jnp.float32).reshape(block_row_span, KEY_VALUE_HEADS, queries_per_group, HEAD_SIZE)
        keys_all = jnp.concatenate([lax.dynamic_slice_in_dim(key_padded, first_row_index, span, 1), vert_key], 1)
        values_all = jnp.concatenate([lax.dynamic_slice_in_dim(value_padded, first_row_index, span, 1), vert_value], 1)
        query_pos = first_row_index + jnp.arange(block_row_span, dtype=jnp.int32)
        band_pos = first_row_index - SLASH_KEYS_MAX + jnp.arange(span, dtype=jnp.int32)
        visible = attention_mask(query_pos, band_pos, vertical_positions, band_width_list)
        scores = jnp.einsum('qgad,gkd->gaqk', query_block, keys_all) * score_scale
        filled = jnp.where(visible, scores, NEG_FILL)
        row_top = lax.optimization_barrier(jnp.max(filled, axis=3, keepdims=True))
        row_total = lax.optimization_barrier(jnp.sum(jnp.exp(filled - row_top), axis=3, keepdims=True))
        prob_f32 = jnp.exp(filled - (row_top + jnp.log(row_total)))
        prob_weights = lax.optimization_barrier(prob_f32.astype(jnp.bfloat16)).astype(jnp.float32)
        attn_out = jnp.einsum('gaqk,gkd->qgad', prob_weights, values_all).astype(jnp.bfloat16)
        attn_wide = lax.optimization_barrier(attn_out).astype(jnp.float32)
        row_delta = lax.optimization_barrier(jnp.sum(block_gradient * attn_wide, axis=3)).transpose(1, 2, 0)[..., None]
        grad_prob = jnp.einsum('qgad,gkd->gaqk', block_gradient, values_all)
        grad_score = lax.optimization_barrier((prob_f32 * (grad_prob - row_delta)).astype(jnp.bfloat16)).astype(jnp.float32)
        grad_query = (jnp.einsum('gaqk,gkd->qgad', grad_score, keys_all) * score_scale).astype(jnp.bfloat16)
        grad_key = jnp.einsum('gaqk,qgad->gkd', grad_score, query_block) * score_scale
        grad_value = jnp.einsum('gaqk,qgad->gkd', prob_weights, block_gradient)
        pad_key = lax.dynamic_update_slice_in_dim(pad_key, lax.dynamic_slice_in_dim(pad_key, first_row_index, span, 1) + grad_key[:, :span], first_row_index, 1)
        pad_value = lax.dynamic_update_slice_in_dim(pad_value, lax.dynamic_slice_in_dim(pad_value, first_row_index, span, 1) + grad_value[:, :span], first_row_index, 1)
        acc_key = acc_key + grad_key[:, span:]
        acc_value = acc_value + grad_value[:, span:]
        return ((pad_key, pad_value, acc_key, acc_value), (attn_out, grad_query))
    initial_state = (jnp.zeros((KEY_VALUE_HEADS, SLASH_KEYS_MAX + sequence_count, HEAD_SIZE), jnp.float32), jnp.zeros((KEY_VALUE_HEADS, SLASH_KEYS_MAX + sequence_count, HEAD_SIZE), jnp.float32), jnp.zeros((KEY_VALUE_HEADS, VERTICAL_BLOCKS * BLOCK_POSITIONS, HEAD_SIZE), jnp.float32), jnp.zeros((KEY_VALUE_HEADS, VERTICAL_BLOCKS * BLOCK_POSITIONS, HEAD_SIZE), jnp.float32))
    blocks = jnp.arange(sequence_count // block_row_span, dtype=jnp.int32)
    final_carry, (attn_all, grad_q_all) = lax.scan(step, initial_state, blocks)
    key_head_gradient = final_carry[0][:, SLASH_KEYS_MAX:].at[head_index_list, vertical_positions].add(final_carry[2])
    value_head_gradient = final_carry[1][:, SLASH_KEYS_MAX:].at[head_index_list, vertical_positions].add(final_carry[3])
    attention = attn_all.reshape(sequence_count, QUERY_HEADS * HEAD_SIZE)
    grad_queries = grad_q_all.reshape(sequence_count, QUERY_HEADS * HEAD_SIZE)
    key_gradient_rows = key_head_gradient.transpose(1, 0, 2).reshape(sequence_count, KEY_VALUE_HEADS * HEAD_SIZE).astype(jnp.bfloat16)
    value_gradient_rows = value_head_gradient.transpose(1, 0, 2).reshape(sequence_count, KEY_VALUE_HEADS * HEAD_SIZE).astype(jnp.bfloat16)
    return (attention, grad_queries, key_gradient_rows, value_gradient_rows)
```

```python
import functools
import math

import jax
import jax.numpy as jnp
from jax import lax
from jax.experimental import pallas as pl
from jax.experimental.pallas import tpu as pltpu
from jax.sharding import PartitionSpec as P

D = 128
BAND = 512
GROUP = 4
VERT = 512
KEYS = BAND + D
LANES = GROUP * D
NEG = -1e30
SCALE = 1.0 / math.sqrt(D)
LOG2_SCALE = math.log2(math.e) * SCALE
F32, BF16 = jnp.float32, jnp.bfloat16
MESH = pl.DeviceIdType.MESH


def dot_nt(a, b):
    return lax.dot_general(a, b, (((1,), (1,)), ((), ())), preferred_element_type=F32)


def dot_nn(a, b):
    return lax.dot_general(a, b, (((1,), (0,)), ((), ())), preferred_element_type=F32)


def kernel(
    ctx_n, head_n,
    vertical, width, q_hbm, k_hbm, v_hbm, g_hbm,
    o_hbm, dq_hbm, dk_hbm, dv_hbm,
    qs, gs, own, band, trans, contrib, part1, red1, vert,
    s_sc, p_sc, d_sc, o_sc, dq_sc, gband, gvert, gvert_out, part2, red2, vsum,
    rim_out, rim_in, final,
    load_sem, kv_send, kv_recv, kv_local, rim_sem, rs1_send, rs1_recv, ag1_send, ag1_recv,
    out_sem, rs2_send, rs2_recv, ag2_send, ag2_recv, back_sem, grad_send, grad_recv, grad_local,
):
    ctx = lax.axis_index("ctx")
    head = lax.axis_index("head")
    rows = own.shape[1]
    tiles = rows // D
    piece = VERT // ctx_n
    ctx_at = lambda by: lax.rem(ctx + by + ctx_n, ctx_n)
    head_at = lambda by: lax.rem(head + by + head_n, head_n)
    block = lambda n: pl.ds(pl.multiple_of(n * D, D), D)
    share = lambda n: pl.ds(pl.multiple_of(n * piece, piece), piece)

    loads = []
    for a in range(GROUP):
        cols = slice(a * D, (a + 1) * D)
        loads.append(pltpu.make_async_copy(q_hbm.at[:, :, cols], qs.at[:, cols, :], load_sem.at[0, a]))
        loads.append(pltpu.make_async_copy(g_hbm.at[:, :, cols], gs.at[:, cols, :], load_sem.at[1, a]))
    for c in loads:
        c.start()
    local = []
    for x, src in enumerate((k_hbm, v_hbm)):
        c = pltpu.make_async_copy(src.at[:, block(head)], own.at[x, block(head), :], kv_local.at[x])
        c.start()
        local.append(c)

    barrier = pltpu.get_barrier_semaphore()
    for by in range(1, head_n):
        pl.semaphore_signal(barrier, inc=1, device_id=(ctx, head_at(by)), device_id_type=MESH)
    for by in range(1, ctx_n):
        pl.semaphore_signal(barrier, inc=1, device_id=(ctx_at(by), head), device_id_type=MESH)
    pl.semaphore_wait(barrier, head_n + ctx_n - 2)

    sends = []
    for by in range(1, head_n):
        to = head_at(by)
        for x, src in enumerate((k_hbm, v_hbm)):
            c = pltpu.make_async_remote_copy(
                src.at[:, block(to)], own.at[x, block(head), :], kv_send.at[x, by], kv_recv.at[x, by],
                device_id=(ctx, to), device_id_type=MESH)
            c.start()
            sends.append(c)
    for c in loads:
        c.wait()
    for c in local:
        c.wait()
    for c in sends:
        c.wait_recv()

    rim = pltpu.make_async_remote_copy(
        own.at[:, rows - BAND :, :], band.at[:, :BAND, :], rim_sem.at[0], rim_sem.at[1],
        device_id=(ctx_at(1), head), device_id_type=MESH)
    rim.start()

    first = ctx * tiles
    for j in range(VERT // D):
        which = jnp.full((D, D), vertical[0, j], jnp.int32) - first
        for x in range(2):
            term = jnp.zeros((D, D), F32)
            for n in range(tiles):
                term = jnp.where(which == n, own[x, n * D : (n + 1) * D, :].astype(F32), term)
            contrib[x, j * D : (j + 1) * D, :] = term.astype(BF16)
    scatter = []
    for by in range(1, ctx_n):
        to = ctx_at(by)
        c = pltpu.make_async_remote_copy(
            contrib.at[:, share(to), :], part1.at[by], rs1_send.at[by], rs1_recv.at[by],
            device_id=(to, head), device_id_type=MESH)
        c.start()
        scatter.append(c)
    for x in range(2):
        band[x, BAND:, :] = own[x]
        trans[x, :, BAND : BAND + rows] = own[x].T
    for c in scatter:
        c.wait_recv()
    for x in range(2):
        total = contrib[x, share(ctx), :].astype(F32)
        for by in range(1, ctx_n):
            total = total + part1[by, x].astype(F32)
        red1[x] = total.astype(BF16)
        vert[x, share(ctx), :] = total.astype(BF16)
    gather = []
    for by in range(1, ctx_n):
        c = pltpu.make_async_remote_copy(
            red1, vert.at[:, share(ctx), :], ag1_send.at[by], ag1_recv.at[by],
            device_id=(ctx_at(by), head), device_id_type=MESH)
        c.start()
        gather.append(c)
    gband[...] = jnp.zeros_like(gband)
    gvert[...] = jnp.zeros_like(gvert)
    rim.wait_recv()
    for x in range(2):
        trans[x, :, :BAND] = band[x, :BAND, :].T
    for c in gather:
        c.wait_recv()
    for x in range(2):
        trans[x, :, BAND + rows :] = vert[x].T

    lane = lax.broadcasted_iota(jnp.int32, (1, LANES), 1)
    pos = lane % D
    wide = jnp.full((1, LANES), width[GROUP - 1], jnp.int32)
    for a in range(GROUP - 1):
        wide = jnp.where(lane // D == a, width[a], wide)
    row_band = lax.broadcasted_iota(jnp.int32, (BAND, 1), 0)
    row_block = lax.broadcasted_iota(jnp.int32, (D, 1), 0)

    def tile(t, _):
        start = pl.multiple_of(t * D, D)
        q, g = qs[t], gs[t]
        keys, values = band[0, pl.ds(start, KEYS), :], band[1, pl.ds(start, KEYS), :]
        s_sc[:KEYS] = dot_nt(keys, q)
        s_sc[KEYS:] = dot_nt(vert[0], q)
        low = jnp.maximum(pos + (BAND + 1) - wide, BAND - (ctx * rows + start))
        part = jnp.where(row_band >= low, s_sc[:BAND], NEG)
        s_sc[:BAND] = part
        top = jnp.max(part, axis=0, keepdims=True)
        part = jnp.where(row_block <= pos, s_sc[BAND:KEYS], NEG)
        s_sc[BAND:KEYS] = part
        top = jnp.maximum(top, jnp.max(part, axis=0, keepdims=True))
        last = pos + (ctx * rows + start) - wide
        for j in range(VERT // D):
            here = slice(KEYS + j * D, KEYS + (j + 1) * D)
            part = jnp.where(row_block <= last - vertical[0, j] * D, s_sc[here], NEG)
            s_sc[here] = part
            top = jnp.maximum(top, jnp.max(part, axis=0, keepdims=True))
        probs = jnp.exp2(s_sc[...] * LOG2_SCALE - top * LOG2_SCALE)
        inv = 1.0 / jnp.sum(probs, axis=0, keepdims=True)
        s_sc[...] = probs
        p_sc[...] = (s_sc[...] * inv).astype(BF16)
        seen = pl.ds(start, KEYS)
        out_t = dot_nn(trans[1, :, seen], p_sc[:KEYS]) + dot_nn(trans[1, :, BAND + rows :], p_sc[KEYS:])
        out_t = out_t.astype(BF16)
        delta = jnp.sum(out_t.astype(F32) * g.astype(F32).T, axis=0, keepdims=True)
        out = out_t.T
        for a in range(GROUP):
            o_sc[t, :, a * D : (a + 1) * D] = out[a * D : (a + 1) * D]
        for here, vals in ((slice(0, KEYS), values), (slice(KEYS, KEYS + VERT), vert[1])):
            d_sc[here] = ((s_sc[here] * inv) * (dot_nt(vals, g) - delta)).astype(BF16)
        dq_t = dot_nn(trans[0, :, seen], d_sc[:KEYS]) + dot_nn(trans[0, :, BAND + rows :], d_sc[KEYS:])
        dq = (dq_t * SCALE).astype(BF16).T
        for a in range(GROUP):
            dq_sc[t, :, a * D : (a + 1) * D] = dq[a * D : (a + 1) * D]
        gband[0, seen, :] += dot_nn(d_sc[:KEYS], q)
        gband[1, seen, :] += dot_nn(p_sc[:KEYS], g)
        gvert[0] += dot_nn(d_sc[KEYS:], q)
        gvert[1] += dot_nn(p_sc[KEYS:], g)
        return 0

    lax.fori_loop(0, tiles, tile, 0)

    outs = [
        pltpu.make_async_copy(o_sc, o_hbm, out_sem.at[0]),
        pltpu.make_async_copy(dq_sc, dq_hbm, out_sem.at[1]),
    ]
    for c in outs:
        c.start()

    for x in range(2):
        gvert_out[x] = gvert[x].astype(BF16)
        rim_out[x] = gband[x, :BAND, :].astype(BF16)
    scatter2 = []
    for by in range(1, ctx_n):
        to = ctx_at(by)
        c = pltpu.make_async_remote_copy(
            gvert_out.at[:, share(to), :], part2.at[by], rs2_send.at[by], rs2_recv.at[by],
            device_id=(to, head), device_id_type=MESH)
        c.start()
        scatter2.append(c)
    back = pltpu.make_async_remote_copy(
        rim_out, rim_in, back_sem.at[0], back_sem.at[1],
        device_id=(ctx_at(-1), head), device_id_type=MESH)
    back.start()
    for c in scatter2:
        c.wait_recv()
    for x in range(2):
        total = gvert[x, share(ctx), :]
        for by in range(1, ctx_n):
            total = total + part2[by, x].astype(F32)
        red2[x] = total.astype(BF16)
        vsum[x, share(ctx), :] = total.astype(BF16)
    gather2 = []
    for by in range(1, ctx_n):
        c = pltpu.make_async_remote_copy(
            red2, vsum.at[:, share(ctx), :], ag2_send.at[by], ag2_recv.at[by],
            device_id=(ctx_at(by), head), device_id_type=MESH)
        c.start()
        gather2.append(c)
    back.wait_recv()
    for c in gather2:
        c.wait_recv()

    for n in range(tiles):
        for x in range(2):
            total = gband[x, BAND + n * D : BAND + (n + 1) * D, :]
            if n * D >= rows - BAND:
                edge = n * D - (rows - BAND)
                total = total + rim_in[x, edge : edge + D, :].astype(F32)
            for j in range(VERT // D):
                term = vsum[x, j * D : (j + 1) * D, :].astype(F32)
                which = jnp.full((D, D), vertical[0, j], jnp.int32) - first
                total = total + jnp.where(which == n, term, jnp.zeros_like(term))
            if x == 0:
                total = total * SCALE
            final[x, n] = total.astype(BF16)
    grads = []
    for by in range(1, head_n):
        to = head_at(by)
        for x, dst in enumerate((dk_hbm, dv_hbm)):
            c = pltpu.make_async_remote_copy(
                final.at[x, to], dst.at[:, block(head)], grad_send.at[x, by], grad_recv.at[x, by],
                device_id=(ctx, to), device_id_type=MESH)
            c.start()
            grads.append(c)
    for x, dst in enumerate((dk_hbm, dv_hbm)):
        c = pltpu.make_async_copy(final.at[x, head], dst.at[:, block(head)], grad_local.at[x])
        c.start()
        outs.append(c)
    for c in sends + scatter + gather + scatter2 + gather2 + [rim, back]:
        c.wait_send()
    for c in grads:
        c.wait()
    for c in outs:
        c.wait()


def per_device(ctx_n, head_n, queries, keys, values, grad, vertical, width):
    rows, cols = queries.shape
    tiles = rows // D
    piece = VERT // ctx_n
    any_, smem = pl.BlockSpec(memory_space=pl.ANY), pl.BlockSpec(memory_space=pltpu.SMEM)
    dma = pltpu.SemaphoreType.DMA
    tiled = jax.ShapeDtypeStruct((tiles, D, cols), BF16)
    o, dq, dk, dv = pl.pallas_call(
        functools.partial(kernel, ctx_n, head_n),
        out_shape=(tiled, tiled, jax.ShapeDtypeStruct(keys.shape, BF16), jax.ShapeDtypeStruct(keys.shape, BF16)),
        in_specs=[smem, smem, any_, any_, any_, any_],
        out_specs=[any_] * 4,
        scratch_shapes=[
            pltpu.VMEM((tiles, LANES, D), BF16),
            pltpu.VMEM((tiles, LANES, D), BF16),
            pltpu.VMEM((2, rows, D), BF16),
            pltpu.VMEM((2, BAND + rows, D), BF16),
            pltpu.VMEM((2, D, BAND + rows + VERT), BF16),
            pltpu.VMEM((2, VERT, D), BF16),
            pltpu.VMEM((ctx_n, 2, piece, D), BF16),
            pltpu.VMEM((2, piece, D), BF16),
            pltpu.VMEM((2, VERT, D), BF16),
            pltpu.VMEM((KEYS + VERT, LANES), F32),
            pltpu.VMEM((KEYS + VERT, LANES), BF16),
            pltpu.VMEM((KEYS + VERT, LANES), BF16),
            pltpu.VMEM((tiles, D, LANES), BF16),
            pltpu.VMEM((tiles, D, LANES), BF16),
            pltpu.VMEM((2, BAND + rows, D), F32),
            pltpu.VMEM((2, VERT, D), F32),
            pltpu.VMEM((2, VERT, D), BF16),
            pltpu.VMEM((ctx_n, 2, piece, D), BF16),
            pltpu.VMEM((2, piece, D), BF16),
            pltpu.VMEM((2, VERT, D), BF16),
            pltpu.VMEM((2, BAND, D), BF16),
            pltpu.VMEM((2, BAND, D), BF16),
            pltpu.VMEM((2, tiles, D, D), BF16),
            dma((2, GROUP)),
            dma((2, head_n)), dma((2, head_n)), dma((2,)),
            dma((2,)),
            dma((ctx_n,)), dma((ctx_n,)), dma((ctx_n,)), dma((ctx_n,)),
            dma((2,)),
            dma((ctx_n,)), dma((ctx_n,)), dma((ctx_n,)), dma((ctx_n,)),
            dma((2,)),
            dma((2, head_n)), dma((2, head_n)), dma((2,)),
        ],
        compiler_params=pltpu.CompilerParams(
            collective_id=0, has_side_effects=True, vmem_limit_bytes=56 * 1024 * 1024
        ),
        name="vertical_slash",
    )(vertical, width, queries.reshape(tiles, D, cols), keys, values, grad.reshape(tiles, D, cols))
    return o.reshape(rows, cols), dq.reshape(rows, cols), dk, dv


def solution(mesh):
    return jax.shard_map(
        functools.partial(per_device, mesh.shape["ctx"], mesh.shape["head"]),
        mesh=mesh,
        in_specs=(
            P("ctx", "head"),
            P(("ctx", "head"), None),
            P(("ctx", "head"), None),
            P("ctx", "head"),
            P("head", None),
            P("head"),
        ),
        out_specs=(
            P("ctx", "head"),
            P("ctx", "head"),
            P(("ctx", "head"), None),
            P(("ctx", "head"), None),
        ),
        check_vma=False,
    )
```

```python
import functools
import math

import jax
import jax.numpy as jnp
from jax import lax
from jax.experimental import pallas as pl
from jax.experimental.pallas import tpu as pltpu
from jax.sharding import PartitionSpec as P

D = 128
BAND = 512
GROUP = 4
VERT = 512
KEYS = BAND + D
LANES = GROUP * D
NEG = -1e30
SCALE = 1.0 / math.sqrt(D)
LOG2_SCALE = math.log2(math.e) * SCALE
F32, BF16 = jnp.float32, jnp.bfloat16
MESH = pl.DeviceIdType.MESH


def dot_nt(a, b):
    return lax.dot_general(a, b, (((1,), (1,)), ((), ())), preferred_element_type=F32)


def dot_nn(a, b):
    return lax.dot_general(a, b, (((1,), (0,)), ((), ())), preferred_element_type=F32)


def kernel(
    ctx_n, head_n,
    vertical, width, q_hbm, k_hbm, v_hbm, g_hbm,
    o_hbm, dq_hbm, dk_hbm, dv_hbm,
    qs, gs, own, band, trans, contrib, part1, red1, vert,
    s_sc, p_band, p_vert, d_sc, gt_band, gt_vert, stat, part_t, o_sc, dq_sc,
    gband, gvert, gvert_out, part2, red2, vsum, rim_out, rim_in, final,
    load_sem, kv_send, kv_recv, kv_local, rim_send, rim_recv, rs1_send, rs1_recv, ag1_send, ag1_recv,
    out_sem, rs2_send, rs2_recv, ag2_send, ag2_recv, back_send, back_recv, grad_send, grad_recv, grad_local,
):
    ctx = lax.axis_index("ctx")
    head = lax.axis_index("head")
    rows = own.shape[1]
    tiles = rows // D
    late = BAND // D
    piece = VERT // ctx_n
    slots = VERT // D
    first = ctx * tiles
    ctx_at = lambda by: lax.rem(ctx + by + ctx_n, ctx_n)
    head_at = lambda by: lax.rem(head + by + head_n, head_n)
    block = lambda n: pl.ds(pl.multiple_of(n * D, D), D)
    share = lambda n: pl.ds(pl.multiple_of(n * piece, piece), piece)
    unsent = []

    def to_device(src, dst, send, recv, ctx_to, head_to):
        c = pltpu.make_async_remote_copy(
            src, dst, send, recv, device_id=(ctx_to, head_to), device_id_type=MESH)
        c.start()
        unsent.append(c)
        return c

    loads = []
    for a in range(GROUP):
        cols = slice(a * D, (a + 1) * D)
        loads.append(pltpu.make_async_copy(q_hbm.at[:, :, cols], qs.at[:, cols, :], load_sem.at[0, a]))
        loads.append(pltpu.make_async_copy(g_hbm.at[:, :, cols], gs.at[:, cols, :], load_sem.at[1, a]))
    sources = (k_hbm, v_hbm)
    local = [
        pltpu.make_async_copy(src.at[:, block(head)], own.at[x, block(head), :], kv_local.at[x])
        for x, src in enumerate(sources)
    ]
    for c in local + loads:
        c.start()

    barrier = pltpu.get_barrier_semaphore()
    for by in range(1, head_n):
        pl.semaphore_signal(barrier, inc=1, device_id=(ctx, head_at(by)), device_id_type=MESH)
    for by in range(1, ctx_n):
        pl.semaphore_signal(barrier, inc=1, device_id=(ctx_at(by), head), device_id_type=MESH)
    pl.semaphore_wait(barrier, head_n + ctx_n - 2)

    arrive = [
        [
            to_device(src.at[:, block(head_at(by))], own.at[x, block(head), :],
                      kv_send.at[x, by], kv_recv.at[x, by], ctx, head_at(by))
            for by in range(1, head_n)
        ]
        for x, src in enumerate(sources)
    ]
    for c in loads + local:
        c.wait()
    gband[...] = jnp.zeros_like(gband)
    gvert[...] = jnp.zeros_like(gvert)
    rim_in[:, : rows - BAND, :] = jnp.zeros((2, rows - BAND, D), BF16)

    def have(x):
        for c in arrive[x]:
            c.wait_recv()
        for j in range(slots):
            which = jnp.full((D, D), vertical[0, j], jnp.int32) - first
            term = jnp.zeros((D, D), F32)
            for n in range(tiles):
                term = jnp.where(which == n, own[x, n * D : (n + 1) * D, :].astype(F32), term)
            contrib[x, j * D : (j + 1) * D, :] = term.astype(BF16)
        terms = [
            to_device(contrib.at[x, share(ctx_at(by)), :], part1.at[x, by],
                      rs1_send.at[x, by], rs1_recv.at[x, by], ctx_at(by), head)
            for by in range(1, ctx_n)
        ]
        rim = to_device(own.at[x, rows - BAND :, :], band.at[x, :BAND, :],
                        rim_send.at[x], rim_recv.at[x], ctx_at(1), head)
        band[x, BAND:, :] = own[x]
        trans[x, :, BAND : BAND + rows] = own[x].T
        return terms, rim

    def spread_sum(x, mine, parts, terms, red, into, send, recv):
        for c in terms:
            c.wait_recv()
        total = mine
        for by in range(1, ctx_n):
            total = total + parts[x, by].astype(F32)
        red[x] = total.astype(BF16)
        into[x, share(ctx), :] = total.astype(BF16)
        return [
            to_device(red.at[x], into.at[x, share(ctx), :], send.at[x, by], recv.at[x, by], ctx_at(by), head)
            for by in range(1, ctx_n)
        ]

    lane = lax.broadcasted_iota(jnp.int32, (1, LANES), 1)
    pos = lane % D
    wide = jnp.full((1, LANES), width[GROUP - 1], jnp.int32)
    for a in range(GROUP - 1):
        wide = jnp.where(lane // D == a, width[a], wide)
    row_band = lax.broadcasted_iota(jnp.int32, (BAND, 1), 0)
    row_block = lax.broadcasted_iota(jnp.int32, (D, 1), 0)
    at_of = lambda t: pl.multiple_of(t * D, D)

    def band_scores(t, _):
        start = at_of(t)
        s_sc[...] = dot_nt(band[0, pl.ds(start, KEYS), :], qs[t])
        low = jnp.maximum(pos + (BAND + 1) - wide, BAND - (ctx * rows + start))
        part = jnp.where(row_band >= low, s_sc[:BAND], NEG)
        s_sc[:BAND] = part
        top = jnp.max(part, axis=0, keepdims=True)
        part = jnp.where(row_block <= pos, s_sc[BAND:], NEG)
        s_sc[BAND:] = part
        top = jnp.maximum(top, jnp.max(part, axis=0, keepdims=True))
        probs = jnp.exp2(s_sc[...] * LOG2_SCALE - top * LOG2_SCALE)
        stat[t, 0:1] = top
        stat[t, 1:2] = jnp.sum(probs, axis=0, keepdims=True)
        p_band[t] = probs.astype(BF16)
        return 0

    def band_out(t, _):
        part_t[t] = dot_nn(trans[1, :, pl.ds(at_of(t), KEYS)], p_band[t])
        return 0

    def vert_scores(t, _):
        s_sc[:VERT] = dot_nt(vert[0], qs[t])
        last = pos + (ctx * rows + at_of(t)) - wide
        top = stat[t, 0:1]
        low = top
        for j in range(slots):
            here = slice(j * D, (j + 1) * D)
            part = jnp.where(row_block <= last - vertical[0, j] * D, s_sc[here], NEG)
            s_sc[here] = part
            top = jnp.maximum(top, jnp.max(part, axis=0, keepdims=True))
        probs = jnp.exp2(s_sc[:VERT] * LOG2_SCALE - top * LOG2_SCALE)
        p_vert[t] = probs.astype(BF16)
        less = jnp.exp2((low - top) * LOG2_SCALE)
        inv = 1.0 / (stat[t, 1:2] * less + jnp.sum(probs, axis=0, keepdims=True))
        stat[t, 2:3] = less * inv
        stat[t, 3:4] = inv
        return 0

    def vert_values(t, _):
        of_band, of_vert = stat[t, 2:3], stat[t, 3:4]
        out_t = part_t[t] * of_band + dot_nn(trans[1, :, BAND + rows :], p_vert[t]) * of_vert
        out_t = out_t.astype(BF16)
        out = out_t.T
        for a in range(GROUP):
            o_sc[t, :, a * D : (a + 1) * D] = out[a * D : (a + 1) * D]
        wide_out = out_t.astype(F32)
        g_t = gs[t].astype(F32).T
        scaled = (g_t * of_vert).astype(BF16)
        gt_vert[t] = scaled
        stat[t, 5:6] = jnp.sum(scaled.astype(F32) * wide_out, axis=0, keepdims=True)
        gvert[1] += dot_nn(p_vert[t], scaled.T)
        scaled = (g_t * of_band).astype(BF16)
        gt_band[t] = scaled
        stat[t, 4:5] = jnp.sum(scaled.astype(F32) * wide_out, axis=0, keepdims=True)
        gs[t] = scaled.T
        return 0

    def vert_keys(t, _):
        d_sc[:VERT] = (p_vert[t].astype(F32) * (dot_nn(vert[1], gt_vert[t]) - stat[t, 5:6])).astype(BF16)
        part_t[t] = dot_nn(trans[0, :, BAND + rows :], d_sc[:VERT])
        gvert[0] += dot_nn(d_sc[:VERT], qs[t])
        return 0

    def band_values(t, _):
        gband[1, pl.ds(at_of(t), KEYS), :] += dot_nn(p_band[t], gs[t])
        return 0

    def band_keys(t, _):
        seen = pl.ds(at_of(t), KEYS)
        d_sc[...] = (p_band[t].astype(F32) * (dot_nn(band[1, seen, :], gt_band[t]) - stat[t, 4:5])).astype(BF16)
        dq = ((part_t[t] + dot_nn(trans[0, :, seen], d_sc[...])) * SCALE).astype(BF16).T
        for a in range(GROUP):
            dq_sc[t, :, a * D : (a + 1) * D] = dq[a * D : (a + 1) * D]
        gband[0, seen, :] += dot_nn(d_sc[...], qs[t])
        return 0

    def run(body, start, stop):
        lax.fori_loop(start, stop, body, 0)

    key_terms, key_rim = have(0)
    run(band_scores, late, tiles)
    value_terms, value_rim = have(1)
    key_rim.wait_recv()
    trans[0, :, :BAND] = band[0, :BAND, :].T
    run(band_scores, 0, late)
    key_all = spread_sum(
        0, contrib[0, share(ctx), :].astype(F32), part1, key_terms, red1, vert, ag1_send, ag1_recv)
    run(band_out, late, tiles)
    value_all = spread_sum(
        1, contrib[1, share(ctx), :].astype(F32), part1, value_terms, red1, vert, ag1_send, ag1_recv)
    value_rim.wait_recv()
    trans[1, :, :BAND] = band[1, :BAND, :].T
    run(band_out, 0, late)
    for c in key_all:
        c.wait_recv()
    trans[0, :, BAND + rows :] = vert[0].T
    run(vert_scores, 0, tiles)
    for c in value_all:
        c.wait_recv()
    trans[1, :, BAND + rows :] = vert[1].T

    def scatter(x):
        gvert_out[x] = gvert[x].astype(BF16)
        return [
            to_device(gvert_out.at[x, share(ctx_at(by)), :], part2.at[x, by],
                      rs2_send.at[x, by], rs2_recv.at[x, by], ctx_at(by), head)
            for by in range(1, ctx_n)
        ]

    def give_rim(x):
        rim_out[x] = gband[x, :BAND, :].astype(BF16)
        return to_device(rim_out.at[x], rim_in.at[x, rows - BAND :, :],
                         back_send.at[x], back_recv.at[x], ctx_at(-1), head)

    run(vert_values, 0, tiles)
    value_terms = scatter(1)
    outs = [pltpu.make_async_copy(o_sc, o_hbm, out_sem.at[0])]
    outs[0].start()
    run(vert_keys, 0, tiles)
    key_terms = scatter(0)
    run(band_values, 0, tiles)
    value_back = give_rim(1)
    value_all = spread_sum(1, gvert[1, share(ctx), :], part2, value_terms, red2, vsum, ag2_send, ag2_recv)
    run(band_keys, 0, late)
    key_back = give_rim(0)
    key_all = spread_sum(0, gvert[0, share(ctx), :], part2, key_terms, red2, vsum, ag2_send, ag2_recv)
    run(band_keys, late, tiles)
    outs.append(pltpu.make_async_copy(dq_sc, dq_hbm, out_sem.at[1]))
    outs[1].start()

    grads = []

    def finish(x, dst, back, everyone):
        back.wait_recv()
        for c in everyone:
            c.wait_recv()
        for by in range(head_n - 1, -1, -1):
            n = head_at(by)
            total = gband[x, pl.ds(pl.multiple_of(BAND + n * D, D), D), :] + rim_in[x, block(n), :].astype(F32)
            for j in range(slots):
                which = jnp.full((D, D), vertical[0, j], jnp.int32) - first
                total = total + jnp.where(which == n, vsum[x, j * D : (j + 1) * D, :].astype(F32), 0.0)
            if x == 0:
                total = total * SCALE
            final[x, by] = total.astype(BF16)
            if by == 0:
                c = pltpu.make_async_copy(final.at[x, by], dst.at[:, block(head)], grad_local.at[x])
                c.start()
                outs.append(c)
            else:
                grads.append(to_device(final.at[x, by], dst.at[:, block(head)],
                                       grad_send.at[x, by], grad_recv.at[x, by], ctx, n))

    finish(1, dv_hbm, value_back, value_all)
    finish(0, dk_hbm, key_back, key_all)
    for c in grads:
        c.wait_recv()
    for c in unsent:
        c.wait_send()
    for c in outs:
        c.wait()


def per_device(ctx_n, head_n, queries, keys, values, grad, vertical, width):
    rows, cols = queries.shape
    tiles = rows // D
    piece = VERT // ctx_n
    any_, smem = pl.BlockSpec(memory_space=pl.ANY), pl.BlockSpec(memory_space=pltpu.SMEM)
    dma = pltpu.SemaphoreType.DMA
    tiled = jax.ShapeDtypeStruct((tiles, D, cols), BF16)
    o, dq, dk, dv = pl.pallas_call(
        functools.partial(kernel, ctx_n, head_n),
        out_shape=(tiled, tiled, jax.ShapeDtypeStruct(keys.shape, BF16), jax.ShapeDtypeStruct(keys.shape, BF16)),
        in_specs=[smem, smem, any_, any_, any_, any_],
        out_specs=[any_] * 4,
        scratch_shapes=[
            pltpu.VMEM((tiles, LANES, D), BF16),
            pltpu.VMEM((tiles, LANES, D), BF16),
            pltpu.VMEM((2, rows, D), BF16),
            pltpu.VMEM((2, BAND + rows, D), BF16),
            pltpu.VMEM((2, D, BAND + rows + VERT), BF16),
            pltpu.VMEM((2, VERT, D), BF16),
            pltpu.VMEM((2, ctx_n, piece, D), BF16),
            pltpu.VMEM((2, piece, D), BF16),
            pltpu.VMEM((2, VERT, D), BF16),
            pltpu.VMEM((KEYS, LANES), F32),
            pltpu.VMEM((tiles, KEYS, LANES), BF16),
            pltpu.VMEM((tiles, VERT, LANES), BF16),
            pltpu.VMEM((KEYS, LANES), BF16),
            pltpu.VMEM((tiles, D, LANES), BF16),
            pltpu.VMEM((tiles, D, LANES), BF16),
            pltpu.VMEM((tiles, 8, LANES), F32),
            pltpu.VMEM((tiles, D, LANES), F32),
            pltpu.VMEM((tiles, D, LANES), BF16),
            pltpu.VMEM((tiles, D, LANES), BF16),
            pltpu.VMEM((2, BAND + rows, D), F32),
            pltpu.VMEM((2, VERT, D), F32),
            pltpu.VMEM((2, VERT, D), BF16),
            pltpu.VMEM((2, ctx_n, piece, D), BF16),
            pltpu.VMEM((2, piece, D), BF16),
            pltpu.VMEM((2, VERT, D), BF16),
            pltpu.VMEM((2, BAND, D), BF16),
            pltpu.VMEM((2, rows, D), BF16),
            pltpu.VMEM((2, head_n, D, D), BF16),
            dma((2, GROUP)),
            dma((2, head_n)), dma((2, head_n)), dma((2,)),
            dma((2,)), dma((2,)),
            dma((2, ctx_n)), dma((2, ctx_n)), dma((2, ctx_n)), dma((2, ctx_n)),
            dma((2,)),
            dma((2, ctx_n)), dma((2, ctx_n)), dma((2, ctx_n)), dma((2, ctx_n)),
            dma((2,)), dma((2,)),
            dma((2, head_n)), dma((2, head_n)), dma((2,)),
        ],
        compiler_params=pltpu.CompilerParams(
            collective_id=0, has_side_effects=True, vmem_limit_bytes=56 * 1024 * 1024
        ),
        name="vertical_slash",
    )(vertical, width, queries.reshape(tiles, D, cols), keys, values, grad.reshape(tiles, D, cols))
    return o.reshape(rows, cols), dq.reshape(rows, cols), dk, dv


def solution(mesh):
    return jax.shard_map(
        functools.partial(per_device, mesh.shape["ctx"], mesh.shape["head"]),
        mesh=mesh,
        in_specs=(
            P("ctx", "head"),
            P(("ctx", "head"), None),
            P(("ctx", "head"), None),
            P("ctx", "head"),
            P("head", None),
            P("head"),
        ),
        out_specs=(
            P("ctx", "head"),
            P("ctx", "head"),
            P(("ctx", "head"), None),
            P(("ctx", "head"), None),
        ),
        check_vma=False,
    )
```

```python
import functools
import math

import jax
import jax.numpy as jnp
from jax import lax
from jax.experimental import pallas as pl
from jax.experimental.pallas import tpu as pltpu
from jax.sharding import PartitionSpec as P

D = 128
BAND = 512
GROUP = 4
VERT = 512
KEYS = BAND + D
LANES = GROUP * D
NEG = -1e30
SCALE = 1.0 / math.sqrt(D)
LOG2_SCALE = math.log2(math.e) * SCALE
F32, BF16 = jnp.float32, jnp.bfloat16
MESH = pl.DeviceIdType.MESH


def dot_nt(a, b):
    return lax.dot_general(a, b, (((1,), (1,)), ((), ())), preferred_element_type=F32)


def dot_nn(a, b):
    return lax.dot_general(a, b, (((1,), (0,)), ((), ())), preferred_element_type=F32)


def kernel(
    ctx_n, head_n,
    vertical_hbm, width_hbm, q_hbm, k_hbm, v_hbm, g_hbm,
    o_hbm, dq_hbm, dk_hbm, dv_hbm,
    qs, gs, own, band, trans, contrib, part1, red1, vert,
    s_sc, p_band, p_vert, d_sc, gt_band, gt_vert, stat, part_t, ot_sc, o_sc, dq_sc,
    gband, gvert, gvert_out, part2, red2, vsum, rim_out, rim_in, final,
    vertical, width, load_sem, kv_send, kv_recv, kv_local, rim_send, rim_recv, rs1_send, rs1_recv, ag1_send, ag1_recv,
    out_sem, rs2_send, rs2_recv, ag2_send, ag2_recv, back_send, back_recv, grad_send, grad_recv, grad_local,
):
    ctx = lax.axis_index("ctx")
    head = lax.axis_index("head")
    rows = own.shape[1]
    tiles = rows // D
    late = BAND // D
    piece = VERT // ctx_n
    slots = VERT // D
    first = ctx * tiles
    ctx_at = lambda by: lax.rem(ctx + by + ctx_n, ctx_n)
    head_at = lambda by: lax.rem(head + by + head_n, head_n)
    block = lambda n: pl.ds(pl.multiple_of(n * D, D), D)
    share = lambda n: pl.ds(pl.multiple_of(n * piece, piece), piece)
    unsent = []

    def to_device(src, dst, send, recv, ctx_to, head_to):
        c = pltpu.make_async_remote_copy(
            src, dst, send, recv, device_id=(ctx_to, head_to), device_id_type=MESH)
        c.start()
        unsent.append(c)
        return c

    loads = [
        pltpu.make_async_copy(vertical_hbm, vertical, load_sem.at[0, GROUP]),
        pltpu.make_async_copy(width_hbm, width, load_sem.at[1, GROUP]),
    ]
    for a in range(GROUP):
        cols = slice(a * D, (a + 1) * D)
        loads.append(pltpu.make_async_copy(q_hbm.at[:, :, cols], qs.at[:, cols, :], load_sem.at[0, a]))
        loads.append(pltpu.make_async_copy(g_hbm.at[:, :, cols], gs.at[:, cols, :], load_sem.at[1, a]))
    sources = (k_hbm, v_hbm)
    local = [
        pltpu.make_async_copy(src.at[:, block(head)], own.at[x, block(head), :], kv_local.at[x])
        for x, src in enumerate(sources)
    ]
    for c in local + loads:
        c.start()

    barrier = pltpu.get_barrier_semaphore()
    for by in range(1, head_n):
        pl.semaphore_signal(barrier, inc=1, device_id=(ctx, head_at(by)), device_id_type=MESH)
    for by in range(1, ctx_n):
        pl.semaphore_signal(barrier, inc=1, device_id=(ctx_at(by), head), device_id_type=MESH)
    pl.semaphore_wait(barrier, head_n + ctx_n - 2)

    def fetch(x):
        return [
            to_device(sources[x].at[:, block(head_at(by))], own.at[x, block(head), :],
                      kv_send.at[x, by], kv_recv.at[x, by], ctx, head_at(by))
            for by in range(1, head_n)
        ]

    arrive = [fetch(0)]
    for c in loads:
        c.wait()
    gband[...] = jnp.zeros_like(gband)
    gvert[...] = jnp.zeros_like(gvert)
    rim_in[:, : rows - BAND, :] = jnp.zeros((2, rows - BAND, D), BF16)
    for c in unsent:
        c.wait_send()
    unsent.clear()
    arrive.append(fetch(1))

    def turn(t, _):
        gt_band[t] = gs[t].T
        return 0

    lax.fori_loop(0, tiles, turn, 0)
    for c in local:
        c.wait()

    def have(x):
        for c in arrive[x]:
            c.wait_recv()
        for j in range(slots):
            which = jnp.full((D, D), vertical[0, j], jnp.int32) - first
            term = jnp.zeros((D, D), F32)
            for n in range(tiles):
                term = jnp.where(which == n, own[x, n * D : (n + 1) * D, :].astype(F32), term)
            contrib[x, j * D : (j + 1) * D, :] = term.astype(BF16)
        terms = [
            to_device(contrib.at[x, share(ctx_at(by)), :], part1.at[x, by],
                      rs1_send.at[x, by], rs1_recv.at[x, by], ctx_at(by), head)
            for by in range(1, ctx_n)
        ]
        rim = to_device(own.at[x, rows - BAND :, :], band.at[x, :BAND, :],
                        rim_send.at[x], rim_recv.at[x], ctx_at(1), head)
        band[x, BAND:, :] = own[x]
        trans[x, :, BAND : BAND + rows] = own[x].T
        return terms, rim

    def spread_sum(x, mine, parts, terms, red, into, send, recv):
        for c in terms:
            c.wait_recv()
        total = mine
        for by in range(1, ctx_n):
            total = total + parts[x, by].astype(F32)
        red[x] = total.astype(BF16)
        into[x, share(ctx), :] = total.astype(BF16)
        return [
            to_device(red.at[x], into.at[x, share(ctx), :], send.at[x, by], recv.at[x, by], ctx_at(by), head)
            for by in range(1, ctx_n)
        ]

    lane = lax.broadcasted_iota(jnp.int32, (1, LANES), 1)
    pos = lane % D
    wide = jnp.full((1, LANES), width[GROUP - 1], jnp.int32)
    for a in range(GROUP - 1):
        wide = jnp.where(lane // D == a, width[a], wide)
    row_band = lax.broadcasted_iota(jnp.int32, (BAND, 1), 0)
    row_block = lax.broadcasted_iota(jnp.int32, (D, 1), 0)
    at_of = lambda t: pl.multiple_of(t * D, D)

    def band_scores(t, _):
        start = at_of(t)
        s_sc[...] = dot_nt(band[0, pl.ds(start, KEYS), :], qs[t])
        low = jnp.maximum(pos + (BAND + 1) - wide, BAND - (ctx * rows + start))
        part = jnp.where(row_band >= low, s_sc[:BAND], NEG)
        s_sc[:BAND] = part
        top = jnp.max(part, axis=0, keepdims=True)
        part = jnp.where(row_block <= pos, s_sc[BAND:], NEG)
        s_sc[BAND:] = part
        top = jnp.maximum(top, jnp.max(part, axis=0, keepdims=True))
        probs = jnp.exp2(s_sc[...] * LOG2_SCALE - top * LOG2_SCALE)
        stat[t, 0:1] = top
        stat[t, 1:2] = jnp.sum(probs, axis=0, keepdims=True)
        p_band[t] = probs.astype(BF16)
        return 0

    def band_out(t, _):
        part_t[t] = dot_nn(trans[1, :, pl.ds(at_of(t), KEYS)], p_band[t])
        return 0

    def vert_scores(t, _):
        s_sc[:VERT] = dot_nt(vert[0], qs[t])
        last = pos + (ctx * rows + at_of(t)) - wide
        top = stat[t, 0:1]
        low = top
        for j in range(slots):
            here = slice(j * D, (j + 1) * D)
            part = jnp.where(row_block <= last - vertical[0, j] * D, s_sc[here], NEG)
            s_sc[here] = part
            top = jnp.maximum(top, jnp.max(part, axis=0, keepdims=True))
        probs = jnp.exp2(s_sc[:VERT] * LOG2_SCALE - top * LOG2_SCALE)
        p_vert[t] = probs.astype(BF16)
        less = jnp.exp2((low - top) * LOG2_SCALE)
        inv = 1.0 / (stat[t, 1:2] * less + jnp.sum(probs, axis=0, keepdims=True))
        stat[t, 2:3] = less * inv
        stat[t, 3:4] = inv
        return 0

    def vert_values(t, _):
        of_band, of_vert = stat[t, 2:3], stat[t, 3:4]
        out_t = part_t[t] * of_band + dot_nn(trans[1, :, BAND + rows :], p_vert[t]) * of_vert
        out_t = out_t.astype(BF16)
        ot_sc[t] = out_t
        scaled = (gt_band[t].astype(F32) * of_vert).astype(BF16)
        gt_vert[t] = scaled
        stat[t, 5:6] = jnp.sum(scaled.astype(F32) * out_t.astype(F32), axis=0, keepdims=True)
        gvert[1] += dot_nn(p_vert[t], scaled.T)
        return 0

    def vert_keys(t, _):
        d_vert = (p_vert[t].astype(F32) * (dot_nn(vert[1], gt_vert[t]) - stat[t, 5:6])).astype(BF16)
        p_vert[t] = d_vert
        gvert[0] += dot_nn(d_vert, qs[t])
        return 0

    def band_values(t, _):
        out_t = ot_sc[t]
        scaled = (gt_band[t].astype(F32) * stat[t, 2:3]).astype(BF16)
        gt_band[t] = scaled
        stat[t, 4:5] = jnp.sum(scaled.astype(F32) * out_t.astype(F32), axis=0, keepdims=True)
        gband[1, pl.ds(at_of(t), KEYS), :] += dot_nn(p_band[t], scaled.T)
        out = out_t.T
        for a in range(GROUP):
            o_sc[t, :, a * D : (a + 1) * D] = out[a * D : (a + 1) * D]
        return 0

    def band_keys(t, _):
        seen = pl.ds(at_of(t), KEYS)
        d_sc[...] = (p_band[t].astype(F32) * (dot_nn(band[1, seen, :], gt_band[t]) - stat[t, 4:5])).astype(BF16)
        dq = dot_nn(trans[0, :, seen], d_sc[...]) + dot_nn(trans[0, :, BAND + rows :], p_vert[t])
        dq = (dq * SCALE).astype(BF16).T
        for a in range(GROUP):
            dq_sc[t, :, a * D : (a + 1) * D] = dq[a * D : (a + 1) * D]
        gband[0, seen, :] += dot_nn(d_sc[...], qs[t])
        return 0

    def run(body, start, stop):
        lax.fori_loop(start, stop, body, 0)

    key_terms, key_rim = have(0)
    run(band_scores, late, tiles)
    value_terms, value_rim = have(1)
    key_rim.wait_recv()
    trans[0, :, :BAND] = band[0, :BAND, :].T
    run(band_scores, 0, late)
    key_all = spread_sum(
        0, contrib[0, share(ctx), :].astype(F32), part1, key_terms, red1, vert, ag1_send, ag1_recv)
    run(band_out, late, tiles)
    value_all = spread_sum(
        1, contrib[1, share(ctx), :].astype(F32), part1, value_terms, red1, vert, ag1_send, ag1_recv)
    value_rim.wait_recv()
    trans[1, :, :BAND] = band[1, :BAND, :].T
    run(band_out, 0, late)
    for c in key_all:
        c.wait_recv()
    trans[0, :, BAND + rows :] = vert[0].T
    run(vert_scores, 0, tiles)
    for c in value_all:
        c.wait_recv()
    trans[1, :, BAND + rows :] = vert[1].T

    def scatter(x):
        gvert_out[x] = gvert[x].astype(BF16)
        return [
            to_device(gvert_out.at[x, share(ctx_at(by)), :], part2.at[x, by],
                      rs2_send.at[x, by], rs2_recv.at[x, by], ctx_at(by), head)
            for by in range(1, ctx_n)
        ]

    def give_rim(x):
        rim_out[x] = gband[x, :BAND, :].astype(BF16)
        return to_device(rim_out.at[x], rim_in.at[x, rows - BAND :, :],
                         back_send.at[x], back_recv.at[x], ctx_at(-1), head)

    half = late // 2
    run(vert_values, 0, tiles)
    value_terms = scatter(1)
    run(vert_keys, 0, tiles)
    key_terms = scatter(0)
    run(band_values, 0, late)
    value_back = give_rim(1)
    value_all = spread_sum(1, gvert[1, share(ctx), :], part2, value_terms, red2, vsum, ag2_send, ag2_recv)
    run(band_values, late, tiles)
    outs = [pltpu.make_async_copy(o_sc, o_hbm, out_sem.at[0])]
    outs[0].start()
    run(band_keys, 0, half)
    key_all = spread_sum(0, gvert[0, share(ctx), :], part2, key_terms, red2, vsum, ag2_send, ag2_recv)
    run(band_keys, half, late)
    key_back = give_rim(0)

    grads = []

    def finish(x, dst, back, everyone):
        back.wait_recv()
        for c in everyone:
            c.wait_recv()
        for by in range(head_n - 1, -1, -1):
            n = head_at(by)
            total = gband[x, pl.ds(pl.multiple_of(BAND + n * D, D), D), :] + rim_in[x, block(n), :].astype(F32)
            for j in range(slots):
                which = jnp.full((D, D), vertical[0, j], jnp.int32) - first
                total = total + jnp.where(which == n, vsum[x, j * D : (j + 1) * D, :].astype(F32), 0.0)
            if x == 0:
                total = total * SCALE
            final[x, by] = total.astype(BF16)
            if by == 0:
                c = pltpu.make_async_copy(final.at[x, by], dst.at[:, block(head)], grad_local.at[x])
                c.start()
                outs.append(c)
            else:
                grads.append(to_device(final.at[x, by], dst.at[:, block(head)],
                                       grad_send.at[x, by], grad_recv.at[x, by], ctx, n))

    most = late + (tiles - late) // 2
    run(band_keys, late, most)
    finish(1, dv_hbm, value_back, value_all)
    run(band_keys, most, tiles)
    finish(0, dk_hbm, key_back, key_all)
    outs.append(pltpu.make_async_copy(dq_sc, dq_hbm, out_sem.at[1]))
    outs[-1].start()
    for c in grads:
        c.wait_recv()
    for c in unsent:
        c.wait_send()
    for c in outs:
        c.wait()


def hand_over(*refs):
    sem = refs[8]
    copies = [pltpu.make_async_copy(refs[i], refs[4 + i], sem.at[i]) for i in range(4)]
    for c in copies:
        c.start()
    for c in copies:
        c.wait()


def per_device(ctx_n, head_n, queries, keys, values, grad, vertical, width):
    rows, cols = queries.shape
    tiles = rows // D
    piece = VERT // ctx_n
    any_ = pl.BlockSpec(memory_space=pl.ANY)
    hbm = pl.BlockSpec(memory_space=pltpu.HBM)
    dma = pltpu.SemaphoreType.DMA
    tiled = jax.ShapeDtypeStruct((tiles, D, cols), BF16)
    results = pl.pallas_call(
        functools.partial(kernel, ctx_n, head_n),
        out_shape=(tiled, tiled, jax.ShapeDtypeStruct(keys.shape, BF16), jax.ShapeDtypeStruct(keys.shape, BF16)),
        in_specs=[hbm] * 6,
        out_specs=[any_] * 4,
        scratch_shapes=[
            pltpu.VMEM((tiles, LANES, D), BF16),
            pltpu.VMEM((tiles, LANES, D), BF16),
            pltpu.VMEM((2, rows, D), BF16),
            pltpu.VMEM((2, BAND + rows, D), BF16),
            pltpu.VMEM((2, D, BAND + rows + VERT), BF16),
            pltpu.VMEM((2, VERT, D), BF16),
            pltpu.VMEM((2, ctx_n, piece, D), BF16),
            pltpu.VMEM((2, piece, D), BF16),
            pltpu.VMEM((2, VERT, D), BF16),
            pltpu.VMEM((KEYS, LANES), F32),
            pltpu.VMEM((tiles, KEYS, LANES), BF16),
            pltpu.VMEM((tiles, VERT, LANES), BF16),
            pltpu.VMEM((KEYS, LANES), BF16),
            pltpu.VMEM((tiles, D, LANES), BF16),
            pltpu.VMEM((tiles, D, LANES), BF16),
            pltpu.VMEM((tiles, 8, LANES), F32),
            pltpu.VMEM((tiles, D, LANES), F32),
            pltpu.VMEM((tiles, D, LANES), BF16),
            pltpu.VMEM((tiles, D, LANES), BF16),
            pltpu.VMEM((tiles, D, LANES), BF16),
            pltpu.VMEM((2, BAND + rows, D), F32),
            pltpu.VMEM((2, VERT, D), F32),
            pltpu.VMEM((2, VERT, D), BF16),
            pltpu.VMEM((2, ctx_n, piece, D), BF16),
            pltpu.VMEM((2, piece, D), BF16),
            pltpu.VMEM((2, VERT, D), BF16),
            pltpu.VMEM((2, BAND, D), BF16),
            pltpu.VMEM((2, rows, D), BF16),
            pltpu.VMEM((2, head_n, D, D), BF16),
            pltpu.SMEM((1, VERT // D), jnp.int32),
            pltpu.SMEM((GROUP,), jnp.int32),
            dma((2, GROUP + 1)),
            dma((2, head_n)), dma((2, head_n)), dma((2,)),
            dma((2,)), dma((2,)),
            dma((2, ctx_n)), dma((2, ctx_n)), dma((2, ctx_n)), dma((2, ctx_n)),
            dma((2,)),
            dma((2, ctx_n)), dma((2, ctx_n)), dma((2, ctx_n)), dma((2, ctx_n)),
            dma((2,)), dma((2,)),
            dma((2, head_n)), dma((2, head_n)), dma((2,)),
        ],
        compiler_params=pltpu.CompilerParams(
            collective_id=0, has_side_effects=True, vmem_limit_bytes=44 * 1024 * 1024
        ),
        name="vertical_slash",
    )(
        *(
            pltpu.with_memory_space_constraint(x, pltpu.HBM)
            for x in (vertical, width, queries.reshape(tiles, D, cols), keys, values, grad.reshape(tiles, D, cols))
        ),
    )
    o, dq, dk, dv = pl.pallas_call(
        hand_over,
        out_shape=tuple(jax.ShapeDtypeStruct(r.shape, r.dtype) for r in results),
        in_specs=[any_] * 4,
        out_specs=[hbm] * 4,
        scratch_shapes=[dma((4,))],
        compiler_params=pltpu.CompilerParams(vmem_limit_bytes=1024 * 1024),
        name="hand_over",
    )(*results)
    return o.reshape(rows, cols), dq.reshape(rows, cols), dk, dv


def solution(mesh):
    return jax.shard_map(
        functools.partial(per_device, mesh.shape["ctx"], mesh.shape["head"]),
        mesh=mesh,
        in_specs=(
            P("ctx", "head"),
            P(("ctx", "head"), None),
            P(("ctx", "head"), None),
            P("ctx", "head"),
            P("head", None),
            P("head"),
        ),
        out_specs=(
            P("ctx", "head"),
            P("ctx", "head"),
            P(("ctx", "head"), None),
            P(("ctx", "head"), None),
        ),
        check_vma=False,
    )
```

```python
import functools
import math

import jax
import jax.numpy as jnp
from jax import lax
from jax.experimental import pallas as pl
from jax.experimental.pallas import tpu as pltpu
from jax.sharding import PartitionSpec as P

D = 128
BAND = 512
GROUP = 4
VERT = 512
KEYS = BAND + D
LANES = GROUP * D
NEG = -1e30
SCALE = 1.0 / math.sqrt(D)
LOG2_SCALE = math.log2(math.e) * SCALE
F32, BF16 = jnp.float32, jnp.bfloat16
MESH = pl.DeviceIdType.MESH


def dot_nt(a, b):
    return lax.dot_general(a, b, (((1,), (1,)), ((), ())), preferred_element_type=F32)


def dot_nn(a, b):
    return lax.dot_general(a, b, (((1,), (0,)), ((), ())), preferred_element_type=F32)


def kernel(
    ctx_n, head_n,
    vertical_hbm, width_hbm, q_hbm, k_hbm, v_hbm, g_hbm,
    o_hbm, dq_hbm, dk_hbm, dv_hbm,
    qs, gs, own, band, trans, contrib, part1, red1, vert,
    s_sc, s_two, p_band, p_vert, d_sc, gt_band, gt_vert, stat, part_t, ot_sc, o_sc, dq_sc,
    gband, gvert, gvert_out, part2, red2, vsum, rim_out, rim_in, final,
    vertical, width, load_sem, kv_send, kv_recv, kv_local, rim_send, rim_recv, rs1_send, rs1_recv, ag1_send, ag1_recv,
    out_sem, rs2_send, rs2_recv, ag2_send, ag2_recv, back_send, back_recv, grad_send, grad_recv, grad_local,
):
    ctx = lax.axis_index("ctx")
    head = lax.axis_index("head")
    rows = own.shape[1]
    tiles = rows // D
    late = BAND // D
    piece = VERT // ctx_n
    slots = VERT // D
    first = ctx * tiles
    ctx_at = lambda by: lax.rem(ctx + by + ctx_n, ctx_n)
    head_at = lambda by: lax.rem(head + by + head_n, head_n)
    block = lambda n: pl.ds(pl.multiple_of(n * D, D), D)
    share = lambda n: pl.ds(pl.multiple_of(n * piece, piece), piece)
    unsent = []

    def to_device(src, dst, send, recv, ctx_to, head_to):
        c = pltpu.make_async_remote_copy(
            src, dst, send, recv, device_id=(ctx_to, head_to), device_id_type=MESH)
        c.start()
        return c

    def to_head(srcs, dst_of, send, recv, of_all):
        for by in range(1, head_n):
            to_device(srcs(by), dst_of(by), send, recv, ctx, head_at(by))
        unsent.append((of_all, send))
        return of_all, recv

    def to_ctx(srcs, dst_of, send, recv, of_all):
        for by in range(1, ctx_n):
            to_device(srcs(by), dst_of(by), send, recv, ctx_at(by), head)
        unsent.append((of_all, send))
        return of_all, recv

    def drain(of_all_sem):
        of_all, sem = of_all_sem
        pltpu.make_async_copy(of_all, of_all, sem).wait()

    tables = [
        pltpu.make_async_copy(vertical_hbm, vertical, load_sem.at[2]),
        pltpu.make_async_copy(width_hbm, width, load_sem.at[3]),
    ]
    for a in range(GROUP):
        cols = slice(a * D, (a + 1) * D)
        pltpu.make_async_copy(q_hbm.at[:, :, cols], qs.at[:, cols, :], load_sem.at[0]).start()
        pltpu.make_async_copy(g_hbm.at[:, :, cols], gs.at[:, cols, :], load_sem.at[1]).start()
    sources = (k_hbm, v_hbm)
    local = [
        pltpu.make_async_copy(src.at[:, block(head)], own.at[x, block(head), :], kv_local.at[x])
        for x, src in enumerate(sources)
    ]
    for c in local + tables:
        c.start()

    barrier = pltpu.get_barrier_semaphore()
    for by in range(1, head_n):
        pl.semaphore_signal(barrier, inc=1, device_id=(ctx, head_at(by)), device_id_type=MESH)
    for by in range(1, ctx_n):
        pl.semaphore_signal(barrier, inc=1, device_id=(ctx_at(by), head), device_id_type=MESH)
    pl.semaphore_wait(barrier, head_n + ctx_n - 2)

    def fetch(x):
        return to_head(
            lambda by: sources[x].at[:, block(head_at(by))], lambda by: own.at[x, block(head), :],
            kv_send.at[x], kv_recv.at[x], own.at[x, D:, :])

    arrive = [fetch(0)]
    for c in tables:
        c.wait()
    drain((qs, load_sem.at[0]))
    drain((gs, load_sem.at[1]))
    gband[...] = jnp.zeros_like(gband)
    gvert[...] = jnp.zeros_like(gvert)
    rim_in[:, : rows - BAND, :] = jnp.zeros((2, rows - BAND, D), BF16)
    drain(unsent.pop())
    arrive.append(fetch(1))

    def turn(t, _):
        gt_band[t] = gs[t].T
        return 0

    lax.fori_loop(0, tiles, turn, 0)
    for c in local:
        c.wait()

    def have(x):
        drain(arrive[x])
        for j in range(slots):
            which = jnp.full((D, D), vertical[0, j], jnp.int32) - first
            term = jnp.zeros((D, D), F32)
            for n in range(tiles):
                term = jnp.where(which == n, own[x, n * D : (n + 1) * D, :].astype(F32), term)
            contrib[x, j * D : (j + 1) * D, :] = term.astype(BF16)
        terms = to_ctx(
            lambda by: contrib.at[x, share(ctx_at(by)), :], lambda by: part1.at[x, by],
            rs1_send.at[x], rs1_recv.at[x], part1.at[x, 1:])
        rim = to_device(own.at[x, rows - BAND :, :], band.at[x, :BAND, :],
                        rim_send.at[x], rim_recv.at[x], ctx_at(1), head)
        band[x, BAND:, :] = own[x]
        trans[x, :, BAND : BAND + rows] = own[x].T
        return terms, rim

    def spread_sum(x, mine, parts, terms, red, into, send, recv):
        drain(terms)
        total = mine
        for by in range(1, ctx_n):
            total = total + parts[x, by].astype(F32)
        red[x] = total.astype(BF16)
        into[x, share(ctx), :] = total.astype(BF16)
        return to_ctx(
            lambda by: red.at[x], lambda by: into.at[x, share(ctx), :],
            send.at[x], recv.at[x], into.at[x, piece:, :])

    lane = lax.broadcasted_iota(jnp.int32, (1, LANES), 1)
    pos = lane % D
    wide = jnp.full((1, LANES), width[GROUP - 1], jnp.int32)
    for a in range(GROUP - 1):
        wide = jnp.where(lane // D == a, width[a], wide)
    row_band = lax.broadcasted_iota(jnp.int32, (BAND, 1), 0)
    row_block = lax.broadcasted_iota(jnp.int32, (D, 1), 0)
    at_of = lambda t: t * D if isinstance(t, int) else pl.multiple_of(t * D, D)

    def band_scores(t, _):
        start = at_of(t)
        s_sc[...] = dot_nt(band[0, pl.ds(start, KEYS), :], qs[t])
        low = jnp.maximum(pos + (BAND + 1) - wide, BAND - (ctx * rows + start))
        part = jnp.where(row_band >= low, s_sc[:BAND], NEG)
        s_sc[:BAND] = part
        top = jnp.max(part, axis=0, keepdims=True)
        part = jnp.where(row_block <= pos, s_sc[BAND:], NEG)
        s_sc[BAND:] = part
        top = jnp.maximum(top, jnp.max(part, axis=0, keepdims=True))
        probs = jnp.exp2(s_sc[...] * LOG2_SCALE - top * LOG2_SCALE)
        stat[t, 0:1] = top
        stat[t, 1:2] = jnp.sum(probs, axis=0, keepdims=True)
        p_band[t] = probs.astype(BF16)
        return 0

    def band_out(t, _):
        part_t[t] = dot_nn(trans[1, :, pl.ds(at_of(t), KEYS)], p_band[t])
        return 0

    def vert_scores(t, _):
        s_sc = s_two.at[t % 2]
        s_sc[...] = dot_nt(vert[0], qs[t])
        last = pos + (ctx * rows + at_of(t)) - wide
        top = stat[t, 0:1]
        low = top
        for j in range(slots):
            here = slice(j * D, (j + 1) * D)
            part = jnp.where(row_block <= last - vertical[0, j] * D, s_sc[here], NEG)
            s_sc[here] = part
            top = jnp.maximum(top, jnp.max(part, axis=0, keepdims=True))
        probs = jnp.exp2(s_sc[...] * LOG2_SCALE - top * LOG2_SCALE)
        p_vert[t] = probs.astype(BF16)
        less = jnp.exp2((low - top) * LOG2_SCALE)
        inv = 1.0 / (stat[t, 1:2] * less + jnp.sum(probs, axis=0, keepdims=True))
        stat[t, 2:3] = less * inv
        stat[t, 3:4] = inv
        return 0

    def vert_values(t, _):
        of_band, of_vert = stat[t, 2:3], stat[t, 3:4]
        out_t = part_t[t] * of_band + dot_nn(trans[1, :, BAND + rows :], p_vert[t]) * of_vert
        out_t = out_t.astype(BF16)
        ot_sc[t] = out_t
        scaled = (gt_band[t].astype(F32) * of_vert).astype(BF16)
        gt_vert[t] = scaled
        stat[t, 5:6] = jnp.sum(scaled.astype(F32) * out_t.astype(F32), axis=0, keepdims=True)
        gvert[1] += dot_nn(p_vert[t], scaled.T)
        return 0

    def vert_keys(t, _):
        d_vert = (p_vert[t].astype(F32) * (dot_nn(vert[1], gt_vert[t]) - stat[t, 5:6])).astype(BF16)
        p_vert[t] = d_vert
        gvert[0] += dot_nn(d_vert, qs[t])
        return 0

    def band_values(t, _):
        out_t = ot_sc[t]
        scaled = (gt_band[t].astype(F32) * stat[t, 2:3]).astype(BF16)
        gt_band[t] = scaled
        stat[t, 4:5] = jnp.sum(scaled.astype(F32) * out_t.astype(F32), axis=0, keepdims=True)
        gband[1, pl.ds(at_of(t), KEYS), :] += dot_nn(p_band[t], scaled.T)
        out = out_t.T
        for a in range(GROUP):
            o_sc[t, :, a * D : (a + 1) * D] = out[a * D : (a + 1) * D]
        return 0

    def band_keys(t, _):
        seen = pl.ds(at_of(t), KEYS)
        d_sc[...] = (p_band[t].astype(F32) * (dot_nn(band[1, seen, :], gt_band[t]) - stat[t, 4:5])).astype(BF16)
        dq = dot_nn(trans[0, :, seen], d_sc[...]) + dot_nn(trans[0, :, BAND + rows :], p_vert[t])
        dq = (dq * SCALE).astype(BF16).T
        for a in range(GROUP):
            dq_sc[t, :, a * D : (a + 1) * D] = dq[a * D : (a + 1) * D]
        gband[0, seen, :] += dot_nn(d_sc[...], qs[t])
        return 0

    def run(body, start, stop):
        lax.fori_loop(start, stop, body, 0)

    key_terms, key_rim = have(0)
    run(band_scores, late, tiles)
    value_terms, value_rim = have(1)
    key_rim.wait_recv()
    trans[0, :, :BAND] = band[0, :BAND, :].T
    run(band_scores, 0, late)
    key_all = spread_sum(
        0, contrib[0, share(ctx), :].astype(F32), part1, key_terms, red1, vert, ag1_send, ag1_recv)
    run(band_out, late, tiles)
    value_all = spread_sum(
        1, contrib[1, share(ctx), :].astype(F32), part1, value_terms, red1, vert, ag1_send, ag1_recv)
    value_rim.wait_recv()
    trans[1, :, :BAND] = band[1, :BAND, :].T
    run(band_out, 0, late)
    drain(key_all)
    trans[0, :, BAND + rows :] = vert[0].T
    drain(value_all)
    trans[1, :, BAND + rows :] = vert[1].T

    def scatter(x):
        gvert_out[x] = gvert[x].astype(BF16)
        return to_ctx(
            lambda by: gvert_out.at[x, share(ctx_at(by)), :], lambda by: part2.at[x, by],
            rs2_send.at[x], rs2_recv.at[x], part2.at[x, 1:])

    def give_rim(x):
        rim_out[x] = gband[x, :BAND, :].astype(BF16)
        return to_device(rim_out.at[x], rim_in.at[x, rows - BAND :, :],
                         back_send.at[x], back_recv.at[x], ctx_at(-1), head)

    half = late // 2
    for t in range(tiles + 1):
        if t < tiles:
            vert_scores(t, 0)
        if t > 0:
            vert_values(t - 1, 0)
    value_terms = scatter(1)
    for t in range(tiles):
        vert_keys(t, 0)
    key_terms = scatter(0)
    run(band_values, 0, late)
    value_back = give_rim(1)
    value_all = spread_sum(1, gvert[1, share(ctx), :], part2, value_terms, red2, vsum, ag2_send, ag2_recv)
    run(band_values, late, tiles)
    outs = [pltpu.make_async_copy(o_sc, o_hbm, out_sem.at[0])]
    outs[0].start()
    run(band_keys, 0, half)
    key_all = spread_sum(0, gvert[0, share(ctx), :], part2, key_terms, red2, vsum, ag2_send, ag2_recv)
    run(band_keys, half, late)
    key_back = give_rim(0)

    grads = []

    def finish(x, dst, back, everyone):
        back.wait_recv()
        drain(everyone)
        for by in range(head_n - 1, -1, -1):
            n = head_at(by)
            total = gband[x, pl.ds(pl.multiple_of(BAND + n * D, D), D), :] + rim_in[x, block(n), :].astype(F32)
            for j in range(slots):
                which = jnp.full((D, D), vertical[0, j], jnp.int32) - first
                total = total + jnp.where(which == n, vsum[x, j * D : (j + 1) * D, :].astype(F32), 0.0)
            if x == 0:
                total = total * SCALE
            final[x, by] = total.astype(BF16)
            if by == 0:
                c = pltpu.make_async_copy(final.at[x, by], dst.at[:, block(head)], grad_local.at[x])
                c.start()
                outs.append(c)
            else:
                to_device(final.at[x, by], dst.at[:, block(head)], grad_send.at[x], grad_recv.at[x], ctx, n)
        unsent.append((final.at[x, 1:], grad_send.at[x]))
        grads.append((final.at[x, 1:], grad_recv.at[x]))

    most = late + (tiles - late) // 2
    run(band_keys, late, most)
    finish(1, dv_hbm, value_back, value_all)
    run(band_keys, most, tiles)
    finish(0, dk_hbm, key_back, key_all)
    outs.append(pltpu.make_async_copy(dq_sc, dq_hbm, out_sem.at[1]))
    outs[-1].start()
    for c in grads + unsent:
        drain(c)
    for c in (key_rim, value_rim, key_back, value_back):
        c.wait_send()
    for c in outs:
        c.wait()


def hand_over(*refs):
    sem = refs[8]
    copies = [pltpu.make_async_copy(refs[i], refs[4 + i], sem.at[i]) for i in range(4)]
    for c in copies:
        c.start()
    for c in copies:
        c.wait()


def per_device(ctx_n, head_n, queries, keys, values, grad, vertical, width):
    rows, cols = queries.shape
    tiles = rows // D
    piece = VERT // ctx_n
    any_ = pl.BlockSpec(memory_space=pl.ANY)
    hbm = pl.BlockSpec(memory_space=pltpu.HBM)
    dma = pltpu.SemaphoreType.DMA
    tiled = jax.ShapeDtypeStruct((tiles, D, cols), BF16)
    results = pl.pallas_call(
        functools.partial(kernel, ctx_n, head_n),
        out_shape=(tiled, tiled, jax.ShapeDtypeStruct(keys.shape, BF16), jax.ShapeDtypeStruct(keys.shape, BF16)),
        in_specs=[hbm] * 6,
        out_specs=[any_] * 4,
        scratch_shapes=[
            pltpu.VMEM((tiles, LANES, D), BF16),
            pltpu.VMEM((tiles, LANES, D), BF16),
            pltpu.VMEM((2, rows, D), BF16),
            pltpu.VMEM((2, BAND + rows, D), BF16),
            pltpu.VMEM((2, D, BAND + rows + VERT), BF16),
            pltpu.VMEM((2, VERT, D), BF16),
            pltpu.VMEM((2, ctx_n, piece, D), BF16),
            pltpu.VMEM((2, piece, D), BF16),
            pltpu.VMEM((2, VERT, D), BF16),
            pltpu.VMEM((KEYS, LANES), F32),
            pltpu.VMEM((2, VERT, LANES), F32),
            pltpu.VMEM((tiles, KEYS, LANES), BF16),
            pltpu.VMEM((tiles, VERT, LANES), BF16),
            pltpu.VMEM((KEYS, LANES), BF16),
            pltpu.VMEM((tiles, D, LANES), BF16),
            pltpu.VMEM((tiles, D, LANES), BF16),
            pltpu.VMEM((tiles, 8, LANES), F32),
            pltpu.VMEM((tiles, D, LANES), F32),
            pltpu.VMEM((tiles, D, LANES), BF16),
            pltpu.VMEM((tiles, D, LANES), BF16),
            pltpu.VMEM((tiles, D, LANES), BF16),
            pltpu.VMEM((2, BAND + rows, D), F32),
            pltpu.VMEM((2, VERT, D), F32),
            pltpu.VMEM((2, VERT, D), BF16),
            pltpu.VMEM((2, ctx_n, piece, D), BF16),
            pltpu.VMEM((2, piece, D), BF16),
            pltpu.VMEM((2, VERT, D), BF16),
            pltpu.VMEM((2, BAND, D), BF16),
            pltpu.VMEM((2, rows, D), BF16),
            pltpu.VMEM((2, head_n, D, D), BF16),
            pltpu.SMEM((1, VERT // D), jnp.int32),
            pltpu.SMEM((GROUP,), jnp.int32),
            dma((4,)),
            *[dma((2,))] * 3,
            *[dma((2,))] * 2,
            *[dma((2,))] * 4,
            dma((2,)),
            *[dma((2,))] * 4,
            *[dma((2,))] * 2,
            *[dma((2,))] * 3,
        ],
        compiler_params=pltpu.CompilerParams(
            collective_id=0, has_side_effects=True, vmem_limit_bytes=44 * 1024 * 1024
        ),
        name="vertical_slash",
    )(
        *(
            pltpu.with_memory_space_constraint(x, pltpu.HBM)
            for x in (vertical, width, queries.reshape(tiles, D, cols), keys, values, grad.reshape(tiles, D, cols))
        ),
    )
    o, dq, dk, dv = pl.pallas_call(
        hand_over,
        out_shape=tuple(jax.ShapeDtypeStruct(r.shape, r.dtype) for r in results),
        in_specs=[any_] * 4,
        out_specs=[hbm] * 4,
        scratch_shapes=[dma((4,))],
        compiler_params=pltpu.CompilerParams(vmem_limit_bytes=1024 * 1024),
        name="hand_over",
    )(*results)
    return o.reshape(rows, cols), dq.reshape(rows, cols), dk, dv


def solution(mesh):
    return jax.shard_map(
        functools.partial(per_device, mesh.shape["ctx"], mesh.shape["head"]),
        mesh=mesh,
        in_specs=(
            P("ctx", "head"),
            P(("ctx", "head"), None),
            P(("ctx", "head"), None),
            P("ctx", "head"),
            P("head", None),
            P("head"),
        ),
        out_specs=(
            P("ctx", "head"),
            P("ctx", "head"),
            P(("ctx", "head"), None),
            P(("ctx", "head"), None),
        ),
        check_vma=False,
    )
```

```python
import functools
import math

import jax
import jax.numpy as jnp
from jax import lax
from jax.experimental import pallas as pl
from jax.experimental.pallas import tpu as pltpu
from jax.sharding import PartitionSpec as P

D = 128
BAND = 512
GROUP = 4
VERT = 512
KEYS = BAND + D
LANES = GROUP * D
NEG = -1e30
SCALE = 1.0 / math.sqrt(D)
LOG2_SCALE = math.log2(math.e) * SCALE
F32, BF16 = jnp.float32, jnp.bfloat16
MESH = pl.DeviceIdType.MESH


def dot_nt(a, b):
    return lax.dot_general(a, b, (((1,), (1,)), ((), ())), preferred_element_type=F32)


def dot_nn(a, b):
    return lax.dot_general(a, b, (((1,), (0,)), ((), ())), preferred_element_type=F32)


def kernel(
    ctx_n, head_n,
    vertical_hbm, width_hbm, q_hbm, k_hbm, v_hbm, g_hbm,
    o_hbm, dq_hbm, dk_hbm, dv_hbm,
    qs, gs, kv_in, own, band, trans, contrib, part1, red1, vert,
    s_band, s_vert, p_band, p_vert, d_sc, gt_band, gt_vert, stat, part_t, ot_sc, o_sc, dq_sc,
    gband, gvert, gvert_out, part2, red2, vsum, rim_out, rim_in, final,
    vertical, width, load_sem, kv_send, kv_recv, kv_local, rim_send, rim_recv, rs1_send, rs1_recv, ag1_send, ag1_recv,
    out_sem, rs2_send, rs2_recv, ag2_send, ag2_recv, back_send, back_recv, grad_send, grad_recv, grad_local,
):
    ctx = lax.axis_index("ctx")
    head = lax.axis_index("head")
    rows = own.shape[1]
    tiles = rows // D
    late = BAND // D
    piece = VERT // ctx_n
    slots = VERT // D
    first = ctx * tiles
    ctx_at = lambda by: lax.rem(ctx + by + ctx_n, ctx_n)
    head_at = lambda by: lax.rem(head + by + head_n, head_n)
    block = lambda n: pl.ds(pl.multiple_of(n * D, D), D)
    share = lambda n: pl.ds(pl.multiple_of(n * piece, piece), piece)
    unsent = []

    def to_device(src, dst, send, recv, ctx_to, head_to):
        c = pltpu.make_async_remote_copy(
            src, dst, send, recv, device_id=(ctx_to, head_to), device_id_type=MESH)
        c.start()
        return c

    def to_head(srcs, dst_of, send, recv, of_all):
        for by in range(1, head_n):
            to_device(srcs(by), dst_of(by), send, recv, ctx, head_at(by))
        unsent.append((of_all, send))
        return of_all, recv

    def to_ctx(srcs, dst_of, send, recv, of_all):
        for by in range(1, ctx_n):
            to_device(srcs(by), dst_of(by), send, recv, ctx_at(by), head)
        unsent.append((of_all, send))
        return of_all, recv

    def drain(of_all_sem):
        of_all, sem = of_all_sem
        pltpu.make_async_copy(of_all, of_all, sem).wait()

    tables = [
        pltpu.make_async_copy(vertical_hbm, vertical, load_sem.at[2]),
        pltpu.make_async_copy(width_hbm, width, load_sem.at[3]),
    ]
    for a in range(GROUP):
        cols = slice(a * D, (a + 1) * D)
        pltpu.make_async_copy(q_hbm.at[:, :, cols], qs.at[:, cols, :], load_sem.at[0]).start()
        pltpu.make_async_copy(g_hbm.at[:, :, cols], gs.at[:, cols, :], load_sem.at[1]).start()
    brought = [pltpu.make_async_copy(src, kv_in.at[x], kv_local.at[x]) for x, src in enumerate((k_hbm, v_hbm))]
    for c in brought + tables:
        c.start()

    barrier = pltpu.get_barrier_semaphore()
    for by in range(1, head_n):
        pl.semaphore_signal(barrier, inc=1, device_id=(ctx, head_at(by)), device_id_type=MESH)
    for by in range(1, ctx_n):
        pl.semaphore_signal(barrier, inc=1, device_id=(ctx_at(by), head), device_id_type=MESH)
    pl.semaphore_wait(barrier, head_n + ctx_n - 2)

    def fetch(x):
        return to_head(
            lambda by: kv_in.at[x, :, block(head_at(by))], lambda by: own.at[x, block(head), :],
            kv_send.at[x], kv_recv.at[x], own.at[x, D:, :])

    brought[0].wait()
    arrive = [fetch(0)]
    for c in tables:
        c.wait()
    drain((qs, load_sem.at[0]))
    drain((gs, load_sem.at[1]))
    gband[...] = jnp.zeros_like(gband)
    gvert[...] = jnp.zeros_like(gvert)
    rim_in[:, : rows - BAND, :] = jnp.zeros((2, rows - BAND, D), BF16)
    drain(unsent.pop())
    brought[1].wait()
    arrive.append(fetch(1))

    def turn(t, _):
        gt_band[t] = gs[t].T
        return 0

    lax.fori_loop(0, tiles, turn, 0)
    for x in range(2):
        own[x, block(head), :] = kv_in[x, :, block(head)]

    def have(x):
        drain(arrive[x])
        for j in range(slots):
            which = jnp.full((D, D), vertical[0, j], jnp.int32) - first
            term = jnp.zeros((D, D), F32)
            for n in range(tiles):
                term = jnp.where(which == n, own[x, n * D : (n + 1) * D, :].astype(F32), term)
            contrib[x, j * D : (j + 1) * D, :] = term.astype(BF16)
        terms = to_ctx(
            lambda by: contrib.at[x, share(ctx_at(by)), :], lambda by: part1.at[x, by],
            rs1_send.at[x], rs1_recv.at[x], part1.at[x, 1:])
        band[x, BAND:, :] = own[x]
        trans[x, :, BAND : BAND + rows] = own[x].T
        return terms

    def lend_rim(x):
        return to_device(own.at[x, rows - BAND :, :], band.at[x, :BAND, :],
                         rim_send.at[x], rim_recv.at[x], ctx_at(1), head)

    def take_rim(x, rim):
        rim.wait_recv()
        trans[x, :, :BAND] = band[x, :BAND, :].T

    def spread_sum(x, mine, parts, terms, red, into, send, recv):
        drain(terms)
        total = mine
        for by in range(1, ctx_n):
            total = total + parts[x, by].astype(F32)
        red[x] = total.astype(BF16)
        into[x, share(ctx), :] = total.astype(BF16)
        return to_ctx(
            lambda by: red.at[x], lambda by: into.at[x, share(ctx), :],
            send.at[x], recv.at[x], into.at[x, piece:, :])

    lane = lax.broadcasted_iota(jnp.int32, (1, LANES), 1)
    pos = lane % D
    wide = jnp.full((1, LANES), width[GROUP - 1], jnp.int32)
    for a in range(GROUP - 1):
        wide = jnp.where(lane // D == a, width[a], wide)
    row_block = lax.broadcasted_iota(jnp.int32, (D, 1), 0)
    at_of = lambda t: t * D if isinstance(t, int) else pl.multiple_of(t * D, D)

    def weights(t, blocks, top, held, probs):
        top = jnp.broadcast_to(top, (8, LANES))
        for j, (keys, seen) in enumerate(blocks):
            part = jnp.where(seen, dot_nt(keys, qs[t]), NEG)
            held[j * D : (j + 1) * D] = part
            top = jnp.maximum(top, jnp.max(part.reshape(D // 8, 8, LANES), axis=0))
        top = jnp.max(top, axis=0, keepdims=True)
        total = jnp.zeros((8, LANES), F32)
        for j in range(len(blocks)):
            here = slice(j * D, (j + 1) * D)
            part = jnp.exp2(held[here] * LOG2_SCALE - top * LOG2_SCALE)
            probs[here] = part.astype(BF16)
            total = total + jnp.sum(part.reshape(D // 8, 8, LANES), axis=0)
        return top, jnp.sum(total, axis=0, keepdims=True)

    def band_scores(t, _):
        low = jnp.maximum(pos + (BAND + 1) - wide, BAND - (ctx * rows + t * D))
        blocks = [
            (band[0, (t + j) * D : (t + j + 1) * D, :], row_block >= low - j * D) for j in range(BAND // D)
        ]
        blocks.append((band[0, t * D + BAND : (t + 1) * D + BAND, :], row_block <= pos))
        top, total = weights(t, blocks, NEG, s_band.at[t % 2], p_band.at[t])
        stat[t, 0:1] = top
        stat[t, 1:2] = total
        return 0

    def band_out(t, _):
        part_t[t] = dot_nn(trans[1, :, pl.ds(at_of(t), KEYS)], p_band[t])
        return 0

    def vert_scores(t, _):
        last = pos + (ctx * rows + t * D) - wide
        low = stat[t, 0:1]
        blocks = [
            (vert[0, j * D : (j + 1) * D, :], row_block <= last - vertical[0, j] * D) for j in range(slots)
        ]
        top, total = weights(t, blocks, low, s_vert.at[t % 2], p_vert.at[t])
        less = jnp.exp2((low - top) * LOG2_SCALE)
        inv = 1.0 / (stat[t, 1:2] * less + total)
        stat[t, 2:3] = less * inv
        stat[t, 3:4] = inv
        return 0

    def vert_values(t, _):
        scaled = (gt_band[t].astype(F32) * stat[t, 3:4]).astype(BF16)
        gt_vert[t] = scaled
        gvert[1] += dot_nn(p_vert[t], scaled.T)
        return 0

    def vert_out(t, _):
        of_band, of_vert = stat[t, 2:3], stat[t, 3:4]
        out_t = part_t[t] * of_band + dot_nn(trans[1, :, BAND + rows :], p_vert[t]) * of_vert
        out_t = out_t.astype(BF16)
        ot_sc[t] = out_t
        stat[t, 5:6] = jnp.sum(gt_vert[t].astype(F32) * out_t.astype(F32), axis=0, keepdims=True)
        return 0

    def vert_keys(t, _):
        d_vert = (p_vert[t].astype(F32) * (dot_nn(vert[1], gt_vert[t]) - stat[t, 5:6])).astype(BF16)
        p_vert[t] = d_vert
        gvert[0] += dot_nn(d_vert, qs[t])
        return 0

    def band_values(t, _):
        out_t = ot_sc[t]
        scaled = (gt_band[t].astype(F32) * stat[t, 2:3]).astype(BF16)
        gt_band[t] = scaled
        stat[t, 4:5] = jnp.sum(scaled.astype(F32) * out_t.astype(F32), axis=0, keepdims=True)
        gband[1, pl.ds(at_of(t), KEYS), :] += dot_nn(p_band[t], scaled.T)
        out = out_t.T
        for a in range(GROUP):
            o_sc[t, :, a * D : (a + 1) * D] = out[a * D : (a + 1) * D]
        return 0

    def band_keys(t, _):
        seen = pl.ds(at_of(t), KEYS)
        d_sc[...] = (p_band[t].astype(F32) * (dot_nn(band[1, seen, :], gt_band[t]) - stat[t, 4:5])).astype(BF16)
        dq = dot_nn(trans[0, :, seen], d_sc[...]) + dot_nn(trans[0, :, BAND + rows :], p_vert[t])
        dq = (dq * SCALE).astype(BF16).T
        for a in range(GROUP):
            dq_sc[t, :, a * D : (a + 1) * D] = dq[a * D : (a + 1) * D]
        gband[0, seen, :] += dot_nn(d_sc[...], qs[t])
        return 0

    def run(body, start, stop):
        lax.fori_loop(start, stop, body, 0)

    def scatter(x):
        gvert_out[x] = gvert[x].astype(BF16)
        return to_ctx(
            lambda by: gvert_out.at[x, share(ctx_at(by)), :], lambda by: part2.at[x, by],
            rs2_send.at[x], rs2_recv.at[x], part2.at[x, 1:])

    def give_rim(x):
        rim_out[x] = gband[x, :BAND, :].astype(BF16)
        return to_device(rim_out.at[x], rim_in.at[x, rows - BAND :, :],
                         back_send.at[x], back_recv.at[x], ctx_at(-1), head)

    order = [*range(late, tiles), *range(late)]
    key_terms = have(0)
    for t in range(late, tiles):
        band_scores(t, 0)
    key_rim = lend_rim(0)
    value_terms = have(1)
    run(band_out, late, tiles)
    key_all = spread_sum(
        0, contrib[0, share(ctx), :].astype(F32), part1, key_terms, red1, vert, ag1_send, ag1_recv)
    take_rim(0, key_rim)
    for t in range(late):
        band_scores(t, 0)
    value_all = spread_sum(
        1, contrib[1, share(ctx), :].astype(F32), part1, value_terms, red1, vert, ag1_send, ag1_recv)
    value_rim = lend_rim(1)
    drain(key_all)
    trans[0, :, BAND + rows :] = vert[0].T
    for i in range(tiles + 1):
        if i < tiles:
            vert_scores(order[i], 0)
        if i > 0:
            vert_values(order[i - 1], 0)
    value_terms = scatter(1)
    drain(value_all)
    trans[1, :, BAND + rows :] = vert[1].T

    half = late // 2
    for i, t in enumerate(order):
        if i == tiles - late:
            take_rim(1, value_rim)
        if i >= tiles - late:
            band_out(t, 0)
        vert_out(t, 0)
        vert_keys(t, 0)
    key_terms = scatter(0)
    run(band_values, 0, late)
    value_back = give_rim(1)
    value_all = spread_sum(1, gvert[1, share(ctx), :], part2, value_terms, red2, vsum, ag2_send, ag2_recv)
    run(band_values, late, tiles)
    outs = [pltpu.make_async_copy(o_sc, o_hbm, out_sem.at[0])]
    outs[0].start()
    run(band_keys, 0, half)
    key_all = spread_sum(0, gvert[0, share(ctx), :], part2, key_terms, red2, vsum, ag2_send, ag2_recv)
    run(band_keys, half, late)
    key_back = give_rim(0)

    grads = []

    def finish(x, dst, back, everyone):
        back.wait_recv()
        drain(everyone)
        for by in range(head_n - 1, -1, -1):
            n = head_at(by)
            total = gband[x, pl.ds(pl.multiple_of(BAND + n * D, D), D), :] + rim_in[x, block(n), :].astype(F32)
            for j in range(slots):
                which = jnp.full((D, D), vertical[0, j], jnp.int32) - first
                total = total + jnp.where(which == n, vsum[x, j * D : (j + 1) * D, :].astype(F32), 0.0)
            if x == 0:
                total = total * SCALE
            final[x, by] = total.astype(BF16)
            if by == 0:
                c = pltpu.make_async_copy(final.at[x, by], dst.at[:, block(head)], grad_local.at[x])
                c.start()
                outs.append(c)
            else:
                to_device(final.at[x, by], dst.at[:, block(head)], grad_send.at[x], grad_recv.at[x], ctx, n)
        unsent.append((final.at[x, 1:], grad_send.at[x]))
        grads.append((final.at[x, 1:], grad_recv.at[x]))

    most = late + (tiles - late) // 2
    run(band_keys, late, most)
    finish(1, dv_hbm, value_back, value_all)
    run(band_keys, most, tiles)
    finish(0, dk_hbm, key_back, key_all)
    outs.append(pltpu.make_async_copy(dq_sc, dq_hbm, out_sem.at[1]))
    outs[-1].start()
    for c in grads + unsent:
        drain(c)
    for c in (key_rim, value_rim, key_back, value_back):
        c.wait_send()
    for c in outs:
        c.wait()


def hand_over(*refs):
    sem = refs[8]
    copies = [pltpu.make_async_copy(refs[i], refs[4 + i], sem.at[i]) for i in range(4)]
    for c in copies:
        c.start()
    for c in copies:
        c.wait()


def per_device(ctx_n, head_n, queries, keys, values, grad, vertical, width):
    rows, cols = queries.shape
    tiles = rows // D
    piece = VERT // ctx_n
    any_ = pl.BlockSpec(memory_space=pl.ANY)
    hbm = pl.BlockSpec(memory_space=pltpu.HBM)
    dma = pltpu.SemaphoreType.DMA
    tiled = jax.ShapeDtypeStruct((tiles, D, cols), BF16)
    results = pl.pallas_call(
        functools.partial(kernel, ctx_n, head_n),
        out_shape=(tiled, tiled, jax.ShapeDtypeStruct(keys.shape, BF16), jax.ShapeDtypeStruct(keys.shape, BF16)),
        in_specs=[hbm] * 6,
        out_specs=[any_] * 4,
        scratch_shapes=[
            pltpu.VMEM((tiles, LANES, D), BF16),
            pltpu.VMEM((tiles, LANES, D), BF16),
            pltpu.VMEM((2, *keys.shape), BF16),
            pltpu.VMEM((2, rows, D), BF16),
            pltpu.VMEM((2, BAND + rows, D), BF16),
            pltpu.VMEM((2, D, BAND + rows + VERT), BF16),
            pltpu.VMEM((2, VERT, D), BF16),
            pltpu.VMEM((2, ctx_n, piece, D), BF16),
            pltpu.VMEM((2, piece, D), BF16),
            pltpu.VMEM((2, VERT, D), BF16),
            pltpu.VMEM((2, KEYS, LANES), F32),
            pltpu.VMEM((2, VERT, LANES), F32),
            pltpu.VMEM((tiles, KEYS, LANES), BF16),
            pltpu.VMEM((tiles, VERT, LANES), BF16),
            pltpu.VMEM((KEYS, LANES), BF16),
            pltpu.VMEM((tiles, D, LANES), BF16),
            pltpu.VMEM((tiles, D, LANES), BF16),
            pltpu.VMEM((tiles, 8, LANES), F32),
            pltpu.VMEM((tiles, D, LANES), F32),
            pltpu.VMEM((tiles, D, LANES), BF16),
            pltpu.VMEM((tiles, D, LANES), BF16),
            pltpu.VMEM((tiles, D, LANES), BF16),
            pltpu.VMEM((2, BAND + rows, D), F32),
            pltpu.VMEM((2, VERT, D), F32),
            pltpu.VMEM((2, VERT, D), BF16),
            pltpu.VMEM((2, ctx_n, piece, D), BF16),
            pltpu.VMEM((2, piece, D), BF16),
            pltpu.VMEM((2, VERT, D), BF16),
            pltpu.VMEM((2, BAND, D), BF16),
            pltpu.VMEM((2, rows, D), BF16),
            pltpu.VMEM((2, head_n, D, D), BF16),
            pltpu.SMEM((1, VERT // D), jnp.int32),
            pltpu.SMEM((GROUP,), jnp.int32),
            dma((4,)),
            *[dma((2,))] * 3,
            *[dma((2,))] * 2,
            *[dma((2,))] * 4,
            dma((2,)),
            *[dma((2,))] * 4,
            *[dma((2,))] * 2,
            *[dma((2,))] * 3,
        ],
        compiler_params=pltpu.CompilerParams(
            collective_id=0, has_side_effects=True, vmem_limit_bytes=44 * 1024 * 1024
        ),
        name="vertical_slash",
    )(
        *(
            pltpu.with_memory_space_constraint(x, pltpu.HBM)
            for x in (vertical, width, queries.reshape(tiles, D, cols), keys, values, grad.reshape(tiles, D, cols))
        ),
    )
    o, dq, dk, dv = pl.pallas_call(
        hand_over,
        out_shape=tuple(jax.ShapeDtypeStruct(r.shape, r.dtype) for r in results),
        in_specs=[any_] * 4,
        out_specs=[hbm] * 4,
        scratch_shapes=[dma((4,))],
        compiler_params=pltpu.CompilerParams(vmem_limit_bytes=1024 * 1024),
        name="hand_over",
    )(*results)
    return o.reshape(rows, cols), dq.reshape(rows, cols), dk, dv


def solution(mesh):
    return jax.shard_map(
        functools.partial(per_device, mesh.shape["ctx"], mesh.shape["head"]),
        mesh=mesh,
        in_specs=(
            P("ctx", "head"),
            P(("ctx", "head"), None),
            P(("ctx", "head"), None),
            P("ctx", "head"),
            P("head", None),
            P("head"),
        ),
        out_specs=(
            P("ctx", "head"),
            P("ctx", "head"),
            P(("ctx", "head"), None),
            P(("ctx", "head"), None),
        ),
        check_vma=False,
    )
```

```python
import functools
import math

import jax
import jax.numpy as jnp
from jax import lax
from jax.experimental import pallas as pl
from jax.experimental.pallas import tpu as pltpu
from jax.sharding import PartitionSpec as P

D = 128
BAND = 512
GROUP = 4
VERT = 512
KEYS = BAND + D
LANES = GROUP * D
NEG = -1e30
SCALE = 1.0 / math.sqrt(D)
LOG2_SCALE = math.log2(math.e) * SCALE
F32, BF16 = jnp.float32, jnp.bfloat16
MESH = pl.DeviceIdType.MESH


def dot_nt(a, b):
    return lax.dot_general(a, b, (((1,), (1,)), ((), ())), preferred_element_type=F32)


def dot_nn(a, b):
    return lax.dot_general(a, b, (((1,), (0,)), ((), ())), preferred_element_type=F32)


def kernel(
    ctx_n, head_n,
    vertical_hbm, width_hbm, q_hbm, k_hbm, v_hbm, g_hbm,
    o_hbm, dq_hbm, dk_hbm, dv_hbm,
    qs, gs, q_two, vert_two, hide, kv_in, own, band, trans, contrib, part1, red1, vert,
    s_band, s_vert, p_band, p_vert, d_sc, gt_band, gt_vert, stat, part_t, ot_sc, o_sc, dq_sc,
    gband, gvert, gvert_out, part2, red2, vsum, rim_out, rim_in, final,
    vertical, width, load_sem, kv_send, kv_recv, kv_local, rim_send, rim_recv, rs1_send, rs1_recv, ag1_send, ag1_recv,
    out_sem, rs2_send, rs2_recv, ag2_send, ag2_recv, back_send, back_recv, grad_send, grad_recv, grad_local,
):
    ctx = lax.axis_index("ctx")
    head = lax.axis_index("head")
    rows = own.shape[1]
    tiles = rows // D
    late = BAND // D
    piece = VERT // ctx_n
    slots = VERT // D
    first = ctx * tiles
    ctx_at = lambda by: lax.rem(ctx + by + ctx_n, ctx_n)
    head_at = lambda by: lax.rem(head + by + head_n, head_n)
    block = lambda n: pl.ds(pl.multiple_of(n * D, D), D)
    share = lambda n: pl.ds(pl.multiple_of(n * piece, piece), piece)
    unsent = []
    ctx_offsets = sorted(range(1, ctx_n), key=lambda by: -min(by, ctx_n - by))
    head_offsets = sorted(range(1, head_n), key=lambda by: (-(by % 2), -min(by, head_n - by)))

    def to_device(src, dst, send, recv, ctx_to, head_to):
        c = pltpu.make_async_remote_copy(
            src, dst, send, recv, device_id=(ctx_to, head_to), device_id_type=MESH)
        c.start()
        return c

    def to_head(srcs, dst_of, send, recv, of_all):
        for by in head_offsets:
            to_device(srcs(by), dst_of(by), send, recv, ctx, head_at(by))
        unsent.append((of_all, send))
        return of_all, recv

    def to_ctx(srcs, dst_of, send, recv, of_all):
        for by in ctx_offsets:
            to_device(srcs(by), dst_of(by), send, recv, ctx_at(by), head)
        unsent.append((of_all, send))
        return of_all, recv

    def drain(of_all_sem):
        of_all, sem = of_all_sem
        pltpu.make_async_copy(of_all, of_all, sem).wait()

    tables = [
        pltpu.make_async_copy(vertical_hbm, vertical, load_sem.at[2]),
        pltpu.make_async_copy(width_hbm, width, load_sem.at[3]),
    ]
    for a in range(GROUP):
        cols = slice(a * D, (a + 1) * D)
        pltpu.make_async_copy(q_hbm.at[:, :, cols], qs.at[:, cols, :], load_sem.at[0]).start()
        pltpu.make_async_copy(g_hbm.at[:, :, cols], gs.at[:, cols, :], load_sem.at[1]).start()
    brought = [pltpu.make_async_copy(src, kv_in.at[x], kv_local.at[x]) for x, src in enumerate((k_hbm, v_hbm))]
    for c in brought + tables:
        c.start()

    barrier = pltpu.get_barrier_semaphore()
    for by in head_offsets:
        pl.semaphore_signal(barrier, inc=1, device_id=(ctx, head_at(by)), device_id_type=MESH)
    for by in ctx_offsets:
        pl.semaphore_signal(barrier, inc=1, device_id=(ctx_at(by), head), device_id_type=MESH)
    pl.semaphore_wait(barrier, head_n + ctx_n - 2)

    def fetch(x):
        return to_head(
            lambda by: kv_in.at[x, :, block(head_at(by))], lambda by: own.at[x, block(head), :],
            kv_send.at[x], kv_recv.at[x], own.at[x, D:, :])

    brought[0].wait()
    arrive = [fetch(0)]
    for c in tables:
        c.wait()
    drain((qs, load_sem.at[0]))
    drain((gs, load_sem.at[1]))
    gband[...] = jnp.zeros_like(gband)
    gvert[...] = jnp.zeros_like(gvert)
    rim_in[:, : rows - BAND, :] = jnp.zeros((2, rows - BAND, D), BF16)
    lane = lax.broadcasted_iota(jnp.int32, (1, LANES), 1)
    pos = lane % D
    wide = jnp.full((1, LANES), width[GROUP - 1], jnp.int32)
    for a in range(GROUP - 1):
        wide = jnp.where(lane // D == a, width[a], wide)
    row_block = lax.broadcasted_iota(jnp.int32, (D, 1), 0)

    def prepare(t, _):
        gt_band[t] = gs[t].T
        scaled = qs[t].astype(F32) * LOG2_SCALE
        high = scaled.astype(BF16)
        q_two[t, :, :D] = high
        q_two[t, :, D:] = (scaled - high.astype(F32)).astype(BF16)
        last = pos + (ctx * rows + pl.multiple_of(t * D, D)) - wide
        for j in range(slots):
            hide[t, j * D : (j + 1) * D] = jnp.where(row_block <= last - vertical[0, j] * D, 0.0, NEG)
        return 0

    lax.fori_loop(0, tiles, prepare, 0)
    drain(unsent.pop())
    brought[1].wait()
    arrive.append(fetch(1))

    for x in range(2):
        own[x, block(head), :] = kv_in[x, :, block(head)]

    def have(x):
        drain(arrive[x])
        for j in range(slots):
            which = jnp.full((D, D), vertical[0, j], jnp.int32) - first
            term = jnp.zeros((D, D), F32)
            for n in range(tiles):
                term = jnp.where(which == n, own[x, n * D : (n + 1) * D, :].astype(F32), term)
            contrib[x, j * D : (j + 1) * D, :] = term.astype(BF16)
        terms = to_ctx(
            lambda by: contrib.at[x, share(ctx_at(by)), :], lambda by: part1.at[x, by],
            rs1_send.at[x], rs1_recv.at[x], part1.at[x, 1:])
        band[x, BAND:, :] = own[x]
        trans[x, :, BAND : BAND + rows] = own[x].T
        return terms

    def lend_rim(x):
        return to_device(own.at[x, rows - BAND :, :], band.at[x, :BAND, :],
                         rim_send.at[x], rim_recv.at[x], ctx_at(1), head)

    def take_rim(x, rim):
        rim.wait_recv()
        trans[x, :, :BAND] = band[x, :BAND, :].T

    def spread_sum(x, mine, parts, terms, red, into, send, recv):
        drain(terms)
        total = mine
        for by in range(1, ctx_n):
            total = total + parts[x, by].astype(F32)
        red[x] = total.astype(BF16)
        into[x, share(ctx), :] = total.astype(BF16)
        return to_ctx(
            lambda by: red.at[x], lambda by: into.at[x, share(ctx), :],
            send.at[x], recv.at[x], into.at[x, piece:, :])

    at_of = lambda t: t * D if isinstance(t, int) else pl.multiple_of(t * D, D)

    def weights(t, blocks, held, probs):
        top = jnp.full((8, LANES), NEG, F32)
        for j, (keys, seen) in enumerate(blocks):
            part = jnp.where(seen, dot_nt(keys, qs[t]), NEG)
            held[j * D : (j + 1) * D] = part
            top = jnp.maximum(top, jnp.max(part.reshape(D // 8, 8, LANES), axis=0))
        top = jnp.max(top, axis=0, keepdims=True)
        total = jnp.zeros((8, LANES), F32)
        for j in range(len(blocks)):
            here = slice(j * D, (j + 1) * D)
            part = jnp.exp2(held[here] * LOG2_SCALE - top * LOG2_SCALE)
            probs[here] = part.astype(BF16)
            total = total + jnp.sum(part.reshape(D // 8, 8, LANES), axis=0)
        return top, jnp.sum(total, axis=0, keepdims=True)

    def band_scores(t, _):
        low = jnp.maximum(pos + (BAND + 1) - wide, BAND - (ctx * rows + t * D))
        blocks = [
            (band[0, (t + j) * D : (t + j + 1) * D, :], row_block >= low - j * D) for j in range(BAND // D)
        ]
        blocks.append((band[0, t * D + BAND : (t + 1) * D + BAND, :], row_block <= pos))
        top, total = weights(t, blocks, s_band.at[t % 2], p_band.at[t])
        stat[t, 0:1] = top
        stat[t, 1:2] = total
        return 0

    def band_out(t, _):
        part_t[t] = dot_nn(trans[1, :, pl.ds(at_of(t), KEYS)], p_band[t])
        return 0

    def vert_scores(t, _):
        low = stat[t, 0:1] * LOG2_SCALE
        held, probs = s_vert.at[t % 2], p_vert.at[t]
        top = jnp.broadcast_to(low, (8, LANES))
        for j in range(slots):
            here = slice(j * D, (j + 1) * D)
            part = dot_nt(vert_two[here], q_two[t]) + hide[t, here]
            held[here] = part
            top = jnp.maximum(top, jnp.max(part.reshape(D // 8, 8, LANES), axis=0))
        top = jnp.max(top, axis=0, keepdims=True)
        total = jnp.zeros((8, LANES), F32)
        for j in range(slots):
            here = slice(j * D, (j + 1) * D)
            part = jnp.exp2(held[here] - top)
            probs[here] = part.astype(BF16)
            total = total + jnp.sum(part.reshape(D // 8, 8, LANES), axis=0)
        total = jnp.sum(total, axis=0, keepdims=True)
        less = jnp.exp2(low - top)
        inv = 1.0 / (stat[t, 1:2] * less + total)
        stat[t, 2:3] = less * inv
        stat[t, 3:4] = inv
        return 0

    def vert_values(t, _):
        scaled = (gt_band[t].astype(F32) * stat[t, 3:4]).astype(BF16)
        gt_vert[t] = scaled
        gvert[1] += dot_nn(p_vert[t], scaled.T)
        return 0

    def vert_out(t, _):
        of_band, of_vert = stat[t, 2:3], stat[t, 3:4]
        out_t = part_t[t] * of_band + dot_nn(trans[1, :, BAND + rows :], p_vert[t]) * of_vert
        out_t = out_t.astype(BF16)
        ot_sc[t] = out_t
        stat[t, 5:6] = jnp.sum(gt_vert[t].astype(F32) * out_t.astype(F32), axis=0, keepdims=True)
        return 0

    def vert_keys(t, _):
        d_vert = (p_vert[t].astype(F32) * (dot_nn(vert[1], gt_vert[t]) - stat[t, 5:6])).astype(BF16)
        p_vert[t] = d_vert
        gvert[0] += dot_nn(d_vert, qs[t])
        return 0

    def band_values(t, _):
        out_t = ot_sc[t]
        scaled = (gt_band[t].astype(F32) * stat[t, 2:3]).astype(BF16)
        gt_band[t] = scaled
        stat[t, 4:5] = jnp.sum(scaled.astype(F32) * out_t.astype(F32), axis=0, keepdims=True)
        gband[1, pl.ds(at_of(t), KEYS), :] += dot_nn(p_band[t], scaled.T)
        out = out_t.T
        for a in range(GROUP):
            o_sc[t, :, a * D : (a + 1) * D] = out[a * D : (a + 1) * D]
        return 0

    def band_keys(t, _):
        seen = pl.ds(at_of(t), KEYS)
        d_sc[...] = (p_band[t].astype(F32) * (dot_nn(band[1, seen, :], gt_band[t]) - stat[t, 4:5])).astype(BF16)
        dq = dot_nn(trans[0, :, seen], d_sc[...]) + dot_nn(trans[0, :, BAND + rows :], p_vert[t])
        dq = (dq * SCALE).astype(BF16).T
        for a in range(GROUP):
            dq_sc[t, :, a * D : (a + 1) * D] = dq[a * D : (a + 1) * D]
        gband[0, seen, :] += dot_nn(d_sc[...], qs[t])
        return 0

    def run(body, start, stop):
        lax.fori_loop(start, stop, body, 0)

    def scatter(x):
        gvert_out[x] = gvert[x].astype(BF16)
        return to_ctx(
            lambda by: gvert_out.at[x, share(ctx_at(by)), :], lambda by: part2.at[x, by],
            rs2_send.at[x], rs2_recv.at[x], part2.at[x, 1:])

    def give_rim(x):
        rim_out[x] = gband[x, :BAND, :].astype(BF16)
        return to_device(rim_out.at[x], rim_in.at[x, rows - BAND :, :],
                         back_send.at[x], back_recv.at[x], ctx_at(-1), head)

    order = [*range(late, tiles), *range(late)]
    key_terms = have(0)
    for t in range(late, tiles):
        band_scores(t, 0)
    key_rim = lend_rim(0)
    value_terms = have(1)
    run(band_out, late, tiles)
    key_all = spread_sum(
        0, contrib[0, share(ctx), :].astype(F32), part1, key_terms, red1, vert, ag1_send, ag1_recv)
    take_rim(0, key_rim)
    for t in range(late):
        band_scores(t, 0)
    value_all = spread_sum(
        1, contrib[1, share(ctx), :].astype(F32), part1, value_terms, red1, vert, ag1_send, ag1_recv)
    value_rim = lend_rim(1)
    drain(key_all)
    trans[0, :, BAND + rows :] = vert[0].T
    vert_two[:, :D] = vert[0]
    vert_two[:, D:] = vert[0]
    for i in range(tiles + 1):
        if i < tiles:
            vert_scores(order[i], 0)
        if i > 0:
            vert_values(order[i - 1], 0)
    value_terms = scatter(1)
    drain(value_all)
    trans[1, :, BAND + rows :] = vert[1].T

    half = late // 2
    for i, t in enumerate(order):
        if i == tiles - late:
            take_rim(1, value_rim)
        if i >= tiles - late:
            band_out(t, 0)
        vert_out(t, 0)
        vert_keys(t, 0)
    key_terms = scatter(0)
    run(band_values, 0, late)
    value_back = give_rim(1)
    value_all = spread_sum(1, gvert[1, share(ctx), :], part2, value_terms, red2, vsum, ag2_send, ag2_recv)
    run(band_values, late, tiles)
    outs = [pltpu.make_async_copy(o_sc, o_hbm, out_sem.at[0])]
    outs[0].start()
    run(band_keys, 0, half)
    key_all = spread_sum(0, gvert[0, share(ctx), :], part2, key_terms, red2, vsum, ag2_send, ag2_recv)
    run(band_keys, half, late)
    key_back = give_rim(0)

    grads = []

    def finish(x, dst, back, everyone):
        back.wait_recv()
        drain(everyone)
        for by in (*head_offsets, 0):
            n = head_at(by)
            total = gband[x, pl.ds(pl.multiple_of(BAND + n * D, D), D), :] + rim_in[x, block(n), :].astype(F32)
            for j in range(slots):
                which = jnp.full((D, D), vertical[0, j], jnp.int32) - first
                total = total + jnp.where(which == n, vsum[x, j * D : (j + 1) * D, :].astype(F32), 0.0)
            if x == 0:
                total = total * SCALE
            final[x, by] = total.astype(BF16)
            if by == 0:
                c = pltpu.make_async_copy(final.at[x, by], dst.at[:, block(head)], grad_local.at[x])
                c.start()
                outs.append(c)
            else:
                to_device(final.at[x, by], dst.at[:, block(head)], grad_send.at[x], grad_recv.at[x], ctx, n)
        unsent.append((final.at[x, 1:], grad_send.at[x]))
        grads.append((final.at[x, 1:], grad_recv.at[x]))

    most = late + (tiles - late) // 2
    run(band_keys, late, most)
    finish(1, dv_hbm, value_back, value_all)
    run(band_keys, most, tiles)
    finish(0, dk_hbm, key_back, key_all)
    outs.append(pltpu.make_async_copy(dq_sc, dq_hbm, out_sem.at[1]))
    outs[-1].start()
    for c in grads + unsent:
        drain(c)
    for c in (key_rim, value_rim, key_back, value_back):
        c.wait_send()
    for c in outs:
        c.wait()


def hand_over(*refs):
    sem = refs[8]
    copies = []
    for i in range(4):
        parts = 4 if i < 2 else 2
        step = refs[i].shape[0] // parts
        for p in range(parts):
            here = pl.ds(p * step, step)
            copies.append(pltpu.make_async_copy(refs[i].at[here], refs[4 + i].at[here], sem.at[len(copies)]))
    for c in copies:
        c.start()
    for c in copies:
        c.wait()


def per_device(ctx_n, head_n, queries, keys, values, grad, vertical, width):
    rows, cols = queries.shape
    tiles = rows // D
    piece = VERT // ctx_n
    any_ = pl.BlockSpec(memory_space=pl.ANY)
    hbm = pl.BlockSpec(memory_space=pltpu.HBM)
    dma = pltpu.SemaphoreType.DMA
    tiled = jax.ShapeDtypeStruct((tiles, D, cols), BF16)
    results = pl.pallas_call(
        functools.partial(kernel, ctx_n, head_n),
        out_shape=(tiled, tiled, jax.ShapeDtypeStruct(keys.shape, BF16), jax.ShapeDtypeStruct(keys.shape, BF16)),
        in_specs=[hbm] * 6,
        out_specs=[any_] * 4,
        scratch_shapes=[
            pltpu.VMEM((tiles, LANES, D), BF16),
            pltpu.VMEM((tiles, LANES, D), BF16),
            pltpu.VMEM((tiles, LANES, 2 * D), BF16),
            pltpu.VMEM((VERT, 2 * D), BF16),
            pltpu.VMEM((tiles, VERT, LANES), F32),
            pltpu.VMEM((2, *keys.shape), BF16),
            pltpu.VMEM((2, rows, D), BF16),
            pltpu.VMEM((2, BAND + rows, D), BF16),
            pltpu.VMEM((2, D, BAND + rows + VERT), BF16),
            pltpu.VMEM((2, VERT, D), BF16),
            pltpu.VMEM((2, ctx_n, piece, D), BF16),
            pltpu.VMEM((2, piece, D), BF16),
            pltpu.VMEM((2, VERT, D), BF16),
            pltpu.VMEM((2, KEYS, LANES), F32),
            pltpu.VMEM((2, VERT, LANES), F32),
            pltpu.VMEM((tiles, KEYS, LANES), BF16),
            pltpu.VMEM((tiles, VERT, LANES), BF16),
            pltpu.VMEM((KEYS, LANES), BF16),
            pltpu.VMEM((tiles, D, LANES), BF16),
            pltpu.VMEM((tiles, D, LANES), BF16),
            pltpu.VMEM((tiles, 8, LANES), F32),
            pltpu.VMEM((tiles, D, LANES), F32),
            pltpu.VMEM((tiles, D, LANES), BF16),
            pltpu.VMEM((tiles, D, LANES), BF16),
            pltpu.VMEM((tiles, D, LANES), BF16),
            pltpu.VMEM((2, BAND + rows, D), F32),
            pltpu.VMEM((2, VERT, D), F32),
            pltpu.VMEM((2, VERT, D), BF16),
            pltpu.VMEM((2, ctx_n, piece, D), BF16),
            pltpu.VMEM((2, piece, D), BF16),
            pltpu.VMEM((2, VERT, D), BF16),
            pltpu.VMEM((2, BAND, D), BF16),
            pltpu.VMEM((2, rows, D), BF16),
            pltpu.VMEM((2, head_n, D, D), BF16),
            pltpu.SMEM((1, VERT // D), jnp.int32),
            pltpu.SMEM((GROUP,), jnp.int32),
            dma((4,)),
            *[dma((2,))] * 3,
            *[dma((2,))] * 2,
            *[dma((2,))] * 4,
            dma((2,)),
            *[dma((2,))] * 4,
            *[dma((2,))] * 2,
            *[dma((2,))] * 3,
        ],
        compiler_params=pltpu.CompilerParams(
            collective_id=0, has_side_effects=True, vmem_limit_bytes=44 * 1024 * 1024
        ),
        name="vertical_slash",
    )(
        *(
            pltpu.with_memory_space_constraint(x, pltpu.HBM)
            for x in (vertical, width, queries.reshape(tiles, D, cols), keys, values, grad.reshape(tiles, D, cols))
        ),
    )
    o, dq, dk, dv = pl.pallas_call(
        hand_over,
        out_shape=tuple(jax.ShapeDtypeStruct(r.shape, r.dtype) for r in results),
        in_specs=[any_] * 4,
        out_specs=[hbm] * 4,
        scratch_shapes=[dma((12,))],
        compiler_params=pltpu.CompilerParams(vmem_limit_bytes=1024 * 1024),
        name="hand_over",
    )(*results)
    return o.reshape(rows, cols), dq.reshape(rows, cols), dk, dv


def solution(mesh):
    return jax.shard_map(
        functools.partial(per_device, mesh.shape["ctx"], mesh.shape["head"]),
        mesh=mesh,
        in_specs=(
            P("ctx", "head"),
            P(("ctx", "head"), None),
            P(("ctx", "head"), None),
            P("ctx", "head"),
            P("head", None),
            P("head"),
        ),
        out_specs=(
            P("ctx", "head"),
            P("ctx", "head"),
            P(("ctx", "head"), None),
            P(("ctx", "head"), None),
        ),
        check_vma=False,
    )
```

```python
import functools
import math

import jax
import jax.numpy as jnp
from jax import lax
from jax.experimental import pallas as pl
from jax.experimental.pallas import tpu as pltpu
from jax.sharding import PartitionSpec as P

D = 128
BAND = 512
GROUP = 4
VERT = 512
KEYS = BAND + D
LANES = GROUP * D
NEG = -1e30
SCALE = 1.0 / math.sqrt(D)
LOG2_SCALE = math.log2(math.e) * SCALE
F32, BF16 = jnp.float32, jnp.bfloat16
MESH = pl.DeviceIdType.MESH


def dot_nt(a, b):
    return lax.dot_general(a, b, (((1,), (1,)), ((), ())), preferred_element_type=F32)


def dot_nn(a, b):
    return lax.dot_general(a, b, (((1,), (0,)), ((), ())), preferred_element_type=F32)


def kernel(
    ctx_n, head_n,
    vertical_hbm, width_hbm, q_hbm, k_hbm, v_hbm, g_hbm,
    o_hbm, dq_hbm, dk_hbm, dv_hbm,
    qs, gs, hide, kv_in, own, band, trans, contrib, part1, red1, vert,
    s_band, s_vert, p_band, p_vert, d_sc, gt_band, gt_vert, stat, part_t, ot_sc, o_sc, dq_sc,
    gband, gvert, gvert_out, part2, red2, vsum, rim_out, rim_in, final,
    vertical, width, load_sem, kv_send, kv_recv, kv_local, rim_send, rim_recv, rs1_send, rs1_recv, ag1_send, ag1_recv,
    out_sem, rs2_send, rs2_recv, ag2_send, ag2_recv, back_send, back_recv, grad_send, grad_recv, grad_local,
):
    ctx = lax.axis_index("ctx")
    head = lax.axis_index("head")
    rows = own.shape[1]
    tiles = rows // D
    late = BAND // D
    piece = VERT // ctx_n
    slots = VERT // D
    first = ctx * tiles
    ctx_at = lambda by: lax.rem(ctx + by + ctx_n, ctx_n)
    head_at = lambda by: lax.rem(head + by + head_n, head_n)
    block = lambda n: pl.ds(pl.multiple_of(n * D, D), D)
    share = lambda n: pl.ds(pl.multiple_of(n * piece, piece), piece)
    unsent = []
    ctx_offsets = sorted(range(1, ctx_n), key=lambda by: -min(by, ctx_n - by))
    head_offsets = sorted(range(1, head_n), key=lambda by: (-(by % 2), -min(by, head_n - by)))

    def to_device(src, dst, send, recv, ctx_to, head_to):
        c = pltpu.make_async_remote_copy(
            src, dst, send, recv, device_id=(ctx_to, head_to), device_id_type=MESH)
        c.start()
        return c

    def to_head(srcs, dst_of, send, recv, of_all):
        for by in head_offsets:
            to_device(srcs(by), dst_of(by), send, recv, ctx, head_at(by))
        unsent.append((of_all, send))
        return of_all, recv

    def to_ctx(srcs, dst_of, send, recv, of_all):
        for by in ctx_offsets:
            to_device(srcs(by), dst_of(by), send, recv, ctx_at(by), head)
        unsent.append((of_all, send))
        return of_all, recv

    def drain(of_all_sem):
        of_all, sem = of_all_sem
        pltpu.make_async_copy(of_all, of_all, sem).wait()

    tables = [
        pltpu.make_async_copy(vertical_hbm, vertical, load_sem.at[2]),
        pltpu.make_async_copy(width_hbm, width, load_sem.at[3]),
    ]
    for a in range(GROUP):
        cols = slice(a * D, (a + 1) * D)
        pltpu.make_async_copy(q_hbm.at[:, :, cols], qs.at[:, cols, :], load_sem.at[0]).start()
        pltpu.make_async_copy(g_hbm.at[:, :, cols], gs.at[:, cols, :], load_sem.at[1]).start()
    brought = [pltpu.make_async_copy(src, kv_in.at[x], kv_local.at[x]) for x, src in enumerate((k_hbm, v_hbm))]
    for c in brought + tables:
        c.start()

    barrier = pltpu.get_barrier_semaphore()
    for by in head_offsets:
        pl.semaphore_signal(barrier, inc=1, device_id=(ctx, head_at(by)), device_id_type=MESH)
    for by in ctx_offsets:
        pl.semaphore_signal(barrier, inc=1, device_id=(ctx_at(by), head), device_id_type=MESH)
    pl.semaphore_wait(barrier, head_n + ctx_n - 2)

    def fetch(x):
        return to_head(
            lambda by: kv_in.at[x, :, block(head_at(by))], lambda by: own.at[x, block(head), :],
            kv_send.at[x], kv_recv.at[x], own.at[x, D:, :])

    brought[0].wait()
    arrive = [fetch(0)]
    for c in tables:
        c.wait()
    drain((qs, load_sem.at[0]))
    drain((gs, load_sem.at[1]))
    gband[...] = jnp.zeros_like(gband)
    gvert[...] = jnp.zeros_like(gvert)
    rim_in[:, : rows - BAND, :] = jnp.zeros((2, rows - BAND, D), BF16)
    lane = lax.broadcasted_iota(jnp.int32, (1, LANES), 1)
    pos = lane % D
    wide = jnp.full((1, LANES), width[GROUP - 1], jnp.int32)
    for a in range(GROUP - 1):
        wide = jnp.where(lane // D == a, width[a], wide)
    row_block = lax.broadcasted_iota(jnp.int32, (D, 1), 0)

    def prepare(t, _):
        gt_band[t] = gs[t].T
        last = pos + (ctx * rows + pl.multiple_of(t * D, D)) - wide
        for j in range(slots):
            hide[t, j * D : (j + 1) * D] = jnp.where(row_block <= last - vertical[0, j] * D, 0.0, NEG)
        return 0

    lax.fori_loop(0, tiles, prepare, 0)
    drain(unsent.pop())
    brought[1].wait()
    arrive.append(fetch(1))

    for x in range(2):
        own[x, block(head), :] = kv_in[x, :, block(head)]

    def have(x):
        drain(arrive[x])
        for j in range(slots):
            which = jnp.full((D, D), vertical[0, j], jnp.int32) - first
            term = jnp.zeros((D, D), F32)
            for n in range(tiles):
                term = jnp.where(which == n, own[x, n * D : (n + 1) * D, :].astype(F32), term)
            contrib[x, j * D : (j + 1) * D, :] = term.astype(BF16)
        terms = to_ctx(
            lambda by: contrib.at[x, share(ctx_at(by)), :], lambda by: part1.at[x, by],
            rs1_send.at[x], rs1_recv.at[x], part1.at[x, 1:])
        band[x, BAND:, :] = own[x]
        trans[x, :, BAND : BAND + rows] = own[x].T
        return terms

    def lend_rim(x):
        return to_device(own.at[x, rows - BAND :, :], band.at[x, :BAND, :],
                         rim_send.at[x], rim_recv.at[x], ctx_at(1), head)

    def take_rim(x, rim):
        rim.wait_recv()
        trans[x, :, :BAND] = band[x, :BAND, :].T

    def spread_sum(x, mine, parts, terms, red, into, send, recv):
        drain(terms)
        total = mine
        for by in range(1, ctx_n):
            total = total + parts[x, by].astype(F32)
        red[x] = total.astype(BF16)
        into[x, share(ctx), :] = total.astype(BF16)
        return to_ctx(
            lambda by: red.at[x], lambda by: into.at[x, share(ctx), :],
            send.at[x], recv.at[x], into.at[x, piece:, :])

    at_of = lambda t: t * D if isinstance(t, int) else pl.multiple_of(t * D, D)

    def weights(t, blocks, held, probs):
        top = jnp.full((8, LANES), NEG, F32)
        for j, (keys, seen) in enumerate(blocks):
            part = jnp.where(seen, dot_nt(keys, qs[t]), NEG)
            held[j * D : (j + 1) * D] = part
            top = jnp.maximum(top, jnp.max(part.reshape(D // 8, 8, LANES), axis=0))
        top = jnp.max(top, axis=0, keepdims=True)
        total = jnp.zeros((8, LANES), F32)
        for j in range(len(blocks)):
            here = slice(j * D, (j + 1) * D)
            part = jnp.exp2(held[here] * LOG2_SCALE - top * LOG2_SCALE)
            probs[here] = part.astype(BF16)
            total = total + jnp.sum(part.reshape(D // 8, 8, LANES), axis=0)
        return top, jnp.sum(total, axis=0, keepdims=True)

    def band_scores(t, _):
        low = jnp.maximum(pos + (BAND + 1) - wide, BAND - (ctx * rows + t * D))
        blocks = [
            (band[0, (t + j) * D : (t + j + 1) * D, :], row_block >= low - j * D) for j in range(BAND // D)
        ]
        blocks.append((band[0, t * D + BAND : (t + 1) * D + BAND, :], row_block <= pos))
        top, total = weights(t, blocks, s_band.at[t % 2], p_band.at[t])
        stat[t, 0:1] = top
        stat[t, 1:2] = total
        return 0

    def band_out(t, _):
        part_t[t] = dot_nn(trans[1, :, pl.ds(at_of(t), KEYS)], p_band[t])
        return 0

    def vert_scores(t, _):
        low = stat[t, 0:1]
        held, probs = s_vert.at[t % 2], p_vert.at[t]
        top = jnp.broadcast_to(low, (8, LANES))
        for j in range(slots):
            here = slice(j * D, (j + 1) * D)
            part = dot_nt(vert[0, here], qs[t]) + hide[t, here]
            held[here] = part
            top = jnp.maximum(top, jnp.max(part.reshape(D // 8, 8, LANES), axis=0))
        top = jnp.max(top, axis=0, keepdims=True)
        total = jnp.zeros((8, LANES), F32)
        for j in range(slots):
            here = slice(j * D, (j + 1) * D)
            part = jnp.exp2(held[here] * LOG2_SCALE - top * LOG2_SCALE)
            probs[here] = part.astype(BF16)
            total = total + jnp.sum(part.reshape(D // 8, 8, LANES), axis=0)
        total = jnp.sum(total, axis=0, keepdims=True)
        less = jnp.exp2((low - top) * LOG2_SCALE)
        inv = 1.0 / (stat[t, 1:2] * less + total)
        stat[t, 2:3] = less * inv
        stat[t, 3:4] = inv
        return 0

    def vert_values(t, _):
        scaled = (gt_band[t].astype(F32) * stat[t, 3:4]).astype(BF16)
        gt_vert[t] = scaled
        gvert[1] += dot_nn(p_vert[t], scaled.T)
        return 0

    def vert_out(t, _):
        of_band, of_vert = stat[t, 2:3], stat[t, 3:4]
        out_t = part_t[t] * of_band + dot_nn(trans[1, :, BAND + rows :], p_vert[t]) * of_vert
        out_t = out_t.astype(BF16)
        ot_sc[t] = out_t
        stat[t, 5:6] = jnp.sum(gt_vert[t].astype(F32) * out_t.astype(F32), axis=0, keepdims=True)
        return 0

    def vert_keys(t, _):
        d_vert = (p_vert[t].astype(F32) * (dot_nn(vert[1], gt_vert[t]) - stat[t, 5:6])).astype(BF16)
        p_vert[t] = d_vert
        gvert[0] += dot_nn(d_vert, qs[t])
        return 0

    def band_values(t, _):
        out_t = ot_sc[t]
        scaled = (gt_band[t].astype(F32) * stat[t, 2:3]).astype(BF16)
        gt_band[t] = scaled
        stat[t, 4:5] = jnp.sum(scaled.astype(F32) * out_t.astype(F32), axis=0, keepdims=True)
        gband[1, pl.ds(at_of(t), KEYS), :] += dot_nn(p_band[t], scaled.T)
        out = out_t.T
        for a in range(GROUP):
            o_sc[t, :, a * D : (a + 1) * D] = out[a * D : (a + 1) * D]
        return 0

    def band_keys(t, _):
        seen = pl.ds(at_of(t), KEYS)
        d_sc[...] = (p_band[t].astype(F32) * (dot_nn(band[1, seen, :], gt_band[t]) - stat[t, 4:5])).astype(BF16)
        dq = dot_nn(trans[0, :, seen], d_sc[...]) + dot_nn(trans[0, :, BAND + rows :], p_vert[t])
        dq = (dq * SCALE).astype(BF16).T
        for a in range(GROUP):
            dq_sc[t, :, a * D : (a + 1) * D] = dq[a * D : (a + 1) * D]
        gband[0, seen, :] += dot_nn(d_sc[...], qs[t])
        return 0

    def run(body, start, stop):
        lax.fori_loop(start, stop, body, 0)

    def scatter(x):
        gvert_out[x] = gvert[x].astype(BF16)
        return to_ctx(
            lambda by: gvert_out.at[x, share(ctx_at(by)), :], lambda by: part2.at[x, by],
            rs2_send.at[x], rs2_recv.at[x], part2.at[x, 1:])

    def give_rim(x):
        rim_out[x] = gband[x, :BAND, :].astype(BF16)
        return to_device(rim_out.at[x], rim_in.at[x, rows - BAND :, :],
                         back_send.at[x], back_recv.at[x], ctx_at(-1), head)

    order = [*range(late, tiles), *range(late)]
    key_terms = have(0)
    for t in range(late, tiles):
        band_scores(t, 0)
    key_rim = lend_rim(0)
    value_terms = have(1)
    run(band_out, late, tiles)
    key_all = spread_sum(
        0, contrib[0, share(ctx), :].astype(F32), part1, key_terms, red1, vert, ag1_send, ag1_recv)
    take_rim(0, key_rim)
    for t in range(late):
        band_scores(t, 0)
    value_all = spread_sum(
        1, contrib[1, share(ctx), :].astype(F32), part1, value_terms, red1, vert, ag1_send, ag1_recv)
    value_rim = lend_rim(1)
    drain(key_all)
    trans[0, :, BAND + rows :] = vert[0].T
    for i in range(tiles + 1):
        if i < tiles:
            vert_scores(order[i], 0)
        if i > 0:
            vert_values(order[i - 1], 0)
    value_terms = scatter(1)
    drain(value_all)
    trans[1, :, BAND + rows :] = vert[1].T

    half = late // 2
    for i in range(tiles + 1):
        if i == tiles - late:
            take_rim(1, value_rim)
        if i < tiles:
            if i >= tiles - late:
                band_out(order[i], 0)
            vert_out(order[i], 0)
        if i > 0:
            vert_keys(order[i - 1], 0)
    key_terms = scatter(0)
    run(band_values, 0, late)
    value_back = give_rim(1)
    value_all = spread_sum(1, gvert[1, share(ctx), :], part2, value_terms, red2, vsum, ag2_send, ag2_recv)
    run(band_keys, 0, late)
    key_back = give_rim(0)
    key_all = spread_sum(0, gvert[0, share(ctx), :], part2, key_terms, red2, vsum, ag2_send, ag2_recv)
    run(band_values, late, tiles)
    outs = [pltpu.make_async_copy(o_sc, o_hbm, out_sem.at[0])]
    outs[0].start()

    grads = []

    def finish(x, dst, back, everyone):
        back.wait_recv()
        drain(everyone)
        for by in (*head_offsets, 0):
            n = head_at(by)
            total = gband[x, pl.ds(pl.multiple_of(BAND + n * D, D), D), :] + rim_in[x, block(n), :].astype(F32)
            for j in range(slots):
                which = jnp.full((D, D), vertical[0, j], jnp.int32) - first
                total = total + jnp.where(which == n, vsum[x, j * D : (j + 1) * D, :].astype(F32), 0.0)
            if x == 0:
                total = total * SCALE
            final[x, by] = total.astype(BF16)
            if by == 0:
                c = pltpu.make_async_copy(final.at[x, by], dst.at[:, block(head)], grad_local.at[x])
                c.start()
                outs.append(c)
            else:
                to_device(final.at[x, by], dst.at[:, block(head)], grad_send.at[x], grad_recv.at[x], ctx, n)
        unsent.append((final.at[x, 1:], grad_send.at[x]))
        grads.append((final.at[x, 1:], grad_recv.at[x]))

    most = late + (tiles - late) // 2
    finish(1, dv_hbm, value_back, value_all)
    run(band_keys, late, most)
    run(band_keys, most, tiles)
    finish(0, dk_hbm, key_back, key_all)
    outs.append(pltpu.make_async_copy(dq_sc, dq_hbm, out_sem.at[1]))
    outs[-1].start()
    for c in grads + unsent:
        drain(c)
    for c in (key_rim, value_rim, key_back, value_back):
        c.wait_send()
    for c in outs:
        c.wait()


def hand_over(*refs):
    sem = refs[8]
    copies = []
    for i in range(4):
        parts = 4 if i < 2 else 2
        step = refs[i].shape[0] // parts
        for p in range(parts):
            here = pl.ds(p * step, step)
            copies.append(pltpu.make_async_copy(refs[i].at[here], refs[4 + i].at[here], sem.at[len(copies)]))
    for c in copies:
        c.start()
    for c in copies:
        c.wait()


def per_device(ctx_n, head_n, queries, keys, values, grad, vertical, width):
    rows, cols = queries.shape
    tiles = rows // D
    piece = VERT // ctx_n
    any_ = pl.BlockSpec(memory_space=pl.ANY)
    hbm = pl.BlockSpec(memory_space=pltpu.HBM)
    dma = pltpu.SemaphoreType.DMA
    tiled = jax.ShapeDtypeStruct((tiles, D, cols), BF16)
    results = pl.pallas_call(
        functools.partial(kernel, ctx_n, head_n),
        out_shape=(tiled, tiled, jax.ShapeDtypeStruct(keys.shape, BF16), jax.ShapeDtypeStruct(keys.shape, BF16)),
        in_specs=[hbm] * 6,
        out_specs=[any_] * 4,
        scratch_shapes=[
            pltpu.VMEM((tiles, LANES, D), BF16),
            pltpu.VMEM((tiles, LANES, D), BF16),
            pltpu.VMEM((tiles, VERT, LANES), F32),
            pltpu.VMEM((2, *keys.shape), BF16),
            pltpu.VMEM((2, rows, D), BF16),
            pltpu.VMEM((2, BAND + rows, D), BF16),
            pltpu.VMEM((2, D, BAND + rows + VERT), BF16),
            pltpu.VMEM((2, VERT, D), BF16),
            pltpu.VMEM((2, ctx_n, piece, D), BF16),
            pltpu.VMEM((2, piece, D), BF16),
            pltpu.VMEM((2, VERT, D), BF16),
            pltpu.VMEM((2, KEYS, LANES), F32),
            pltpu.VMEM((2, VERT, LANES), F32),
            pltpu.VMEM((tiles, KEYS, LANES), BF16),
            pltpu.VMEM((tiles, VERT, LANES), BF16),
            pltpu.VMEM((KEYS, LANES), BF16),
            pltpu.VMEM((tiles, D, LANES), BF16),
            pltpu.VMEM((tiles, D, LANES), BF16),
            pltpu.VMEM((tiles, 8, LANES), F32),
            pltpu.VMEM((tiles, D, LANES), F32),
            pltpu.VMEM((tiles, D, LANES), BF16),
            pltpu.VMEM((tiles, D, LANES), BF16),
            pltpu.VMEM((tiles, D, LANES), BF16),
            pltpu.VMEM((2, BAND + rows, D), F32),
            pltpu.VMEM((2, VERT, D), F32),
            pltpu.VMEM((2, VERT, D), BF16),
            pltpu.VMEM((2, ctx_n, piece, D), BF16),
            pltpu.VMEM((2, piece, D), BF16),
            pltpu.VMEM((2, VERT, D), BF16),
            pltpu.VMEM((2, BAND, D), BF16),
            pltpu.VMEM((2, rows, D), BF16),
            pltpu.VMEM((2, head_n, D, D), BF16),
            pltpu.SMEM((1, VERT // D), jnp.int32),
            pltpu.SMEM((GROUP,), jnp.int32),
            dma((4,)),
            *[dma((2,))] * 3,
            *[dma((2,))] * 2,
            *[dma((2,))] * 4,
            dma((2,)),
            *[dma((2,))] * 4,
            *[dma((2,))] * 2,
            *[dma((2,))] * 3,
        ],
        compiler_params=pltpu.CompilerParams(
            collective_id=0, has_side_effects=True, vmem_limit_bytes=44 * 1024 * 1024
        ),
        name="vertical_slash",
    )(
        *(
            pltpu.with_memory_space_constraint(x, pltpu.HBM)
            for x in (vertical, width, queries.reshape(tiles, D, cols), keys, values, grad.reshape(tiles, D, cols))
        ),
    )
    o, dq, dk, dv = pl.pallas_call(
        hand_over,
        out_shape=tuple(jax.ShapeDtypeStruct(r.shape, r.dtype) for r in results),
        in_specs=[any_] * 4,
        out_specs=[hbm] * 4,
        scratch_shapes=[dma((12,))],
        compiler_params=pltpu.CompilerParams(vmem_limit_bytes=1024 * 1024),
        name="hand_over",
    )(*results)
    return o.reshape(rows, cols), dq.reshape(rows, cols), dk, dv


def solution(mesh):
    return jax.shard_map(
        functools.partial(per_device, mesh.shape["ctx"], mesh.shape["head"]),
        mesh=mesh,
        in_specs=(
            P("ctx", "head"),
            P(("ctx", "head"), None),
            P(("ctx", "head"), None),
            P("ctx", "head"),
            P("head", None),
            P("head"),
        ),
        out_specs=(
            P("ctx", "head"),
            P("ctx", "head"),
            P(("ctx", "head"), None),
            P(("ctx", "head"), None),
        ),
        check_vma=False,
    )
```

```python
import functools
import math

import jax
import jax.numpy as jnp
from jax import lax
from jax.experimental import pallas as pl
from jax.experimental.pallas import tpu as pltpu
from jax.sharding import PartitionSpec as P

D = 128
BAND = 512
GROUP = 4
VERT = 512
KEYS = BAND + D
LANES = GROUP * D
NEG = -1e30
SCALE = 1.0 / math.sqrt(D)
LOG2_SCALE = math.log2(math.e) * SCALE
F32, BF16 = jnp.float32, jnp.bfloat16
MESH = pl.DeviceIdType.MESH


def dot_nt(a, b):
    return lax.dot_general(a, b, (((1,), (1,)), ((), ())), preferred_element_type=F32)


def dot_nn(a, b):
    return lax.dot_general(a, b, (((1,), (0,)), ((), ())), preferred_element_type=F32)


def kernel(
    ctx_n, head_n,
    vertical_hbm, width_hbm, q_hbm, k_hbm, v_hbm, g_hbm,
    o_hbm, dq_hbm, dk_hbm, dv_hbm,
    qs, gs, hide, kv_in, own, band, trans, contrib, part1, red1, vert,
    s_band, s_vert, p_band, p_vert, d_sc, gt_band, gt_vert, stat, part_t, ot_sc, o_sc, dq_sc,
    gband, gvert, gvert_out, part2, red2, vsum, rim_out, rim_in, final,
    vertical, width, load_sem, kv_send, kv_recv, kv_local, rim_send, rim_recv, rs1_send, rs1_recv, ag1_send, ag1_recv,
    out_sem, rs2_send, rs2_recv, ag2_send, ag2_recv, back_send, back_recv, grad_send, grad_recv, grad_local,
):
    ctx = lax.axis_index("ctx")
    head = lax.axis_index("head")
    rows = own.shape[1]
    tiles = rows // D
    late = BAND // D
    piece = VERT // ctx_n
    slots = VERT // D
    first = ctx * tiles
    ctx_at = lambda by: lax.rem(ctx + by + ctx_n, ctx_n)
    head_at = lambda by: lax.rem(head + by + head_n, head_n)
    block = lambda n: pl.ds(pl.multiple_of(n * D, D), D)
    share = lambda n: pl.ds(pl.multiple_of(n * piece, piece), piece)
    unsent = []
    ctx_offsets = sorted(range(1, ctx_n), key=lambda by: -min(by, ctx_n - by))
    head_offsets = sorted(range(1, head_n), key=lambda by: (-(by % 2), -min(by, head_n - by)))

    def to_device(src, dst, send, recv, ctx_to, head_to):
        c = pltpu.make_async_remote_copy(
            src, dst, send, recv, device_id=(ctx_to, head_to), device_id_type=MESH)
        c.start()
        return c

    def to_head(srcs, dst_of, send, recv, of_all):
        for by in head_offsets:
            to_device(srcs(by), dst_of(by), send, recv, ctx, head_at(by))
        unsent.append((of_all, send))
        return of_all, recv

    def to_ctx(srcs, dst_of, send, recv, of_all):
        for by in ctx_offsets:
            to_device(srcs(by), dst_of(by), send, recv, ctx_at(by), head)
        unsent.append((of_all, send))
        return of_all, recv

    def drain(of_all_sem):
        of_all, sem = of_all_sem
        pltpu.make_async_copy(of_all, of_all, sem).wait()

    tables = [
        pltpu.make_async_copy(vertical_hbm, vertical, load_sem.at[2]),
        pltpu.make_async_copy(width_hbm, width, load_sem.at[3]),
    ]
    for a in range(GROUP):
        cols = slice(a * D, (a + 1) * D)
        pltpu.make_async_copy(q_hbm.at[:, :, cols], qs.at[:, cols, :], load_sem.at[0]).start()
        pltpu.make_async_copy(g_hbm.at[:, :, cols], gs.at[:, cols, :], load_sem.at[1]).start()
    brought = [pltpu.make_async_copy(src, kv_in.at[x], kv_local.at[x]) for x, src in enumerate((k_hbm, v_hbm))]
    for c in brought + tables:
        c.start()

    barrier = pltpu.get_barrier_semaphore()
    for by in head_offsets:
        pl.semaphore_signal(barrier, inc=1, device_id=(ctx, head_at(by)), device_id_type=MESH)
    for by in ctx_offsets:
        pl.semaphore_signal(barrier, inc=1, device_id=(ctx_at(by), head), device_id_type=MESH)
    pl.semaphore_wait(barrier, head_n + ctx_n - 2)

    def fetch(x):
        return to_head(
            lambda by: kv_in.at[x, :, block(head_at(by))], lambda by: own.at[x, block(head), :],
            kv_send.at[x], kv_recv.at[x], own.at[x, D:, :])

    brought[0].wait()
    arrive = [fetch(0)]
    for c in tables:
        c.wait()
    drain((qs, load_sem.at[0]))
    drain((gs, load_sem.at[1]))
    gband[...] = jnp.zeros_like(gband)
    gvert[...] = jnp.zeros_like(gvert)
    rim_in[:, : rows - BAND, :] = jnp.zeros((2, rows - BAND, D), BF16)
    lane = lax.broadcasted_iota(jnp.int32, (1, LANES), 1)
    pos = lane % D
    wide = jnp.full((1, LANES), width[GROUP - 1], jnp.int32)
    for a in range(GROUP - 1):
        wide = jnp.where(lane // D == a, width[a], wide)
    row_block = lax.broadcasted_iota(jnp.int32, (D, 1), 0)

    def prepare(t, _):
        gt_band[t] = gs[t].T
        last = pos + (ctx * rows + pl.multiple_of(t * D, D)) - wide
        for j in range(slots):
            hide[t, j * D : (j + 1) * D] = jnp.where(row_block <= last - vertical[0, j] * D, 0.0, NEG)
        return 0

    lax.fori_loop(0, tiles, prepare, 0)
    drain(unsent.pop())
    brought[1].wait()
    arrive.append(fetch(1))

    for x in range(2):
        own[x, block(head), :] = kv_in[x, :, block(head)]

    def have(x):
        drain(arrive[x])
        for j in range(slots):
            which = jnp.full((D, D), vertical[0, j], jnp.int32) - first
            term = jnp.zeros((D, D), F32)
            for n in range(tiles):
                term = jnp.where(which == n, own[x, n * D : (n + 1) * D, :].astype(F32), term)
            contrib[x, j * D : (j + 1) * D, :] = term.astype(BF16)
        terms = to_ctx(
            lambda by: contrib.at[x, share(ctx_at(by)), :], lambda by: part1.at[x, by],
            rs1_send.at[x], rs1_recv.at[x], part1.at[x, 1:])
        band[x, BAND:, :] = own[x]
        trans[x, :, BAND : BAND + rows] = own[x].T
        return terms

    def lend_rim(x):
        return to_device(own.at[x, rows - BAND :, :], band.at[x, :BAND, :],
                         rim_send.at[x], rim_recv.at[x], ctx_at(1), head)

    def take_rim(x, rim):
        rim.wait_recv()
        trans[x, :, :BAND] = band[x, :BAND, :].T

    def spread_sum(x, mine, parts, terms, red, into, send, recv):
        drain(terms)
        total = mine
        for by in range(1, ctx_n):
            total = total + parts[x, by].astype(F32)
        red[x] = total.astype(BF16)
        into[x, share(ctx), :] = total.astype(BF16)
        return to_ctx(
            lambda by: red.at[x], lambda by: into.at[x, share(ctx), :],
            send.at[x], recv.at[x], into.at[x, piece:, :])

    at_of = lambda t: t * D if isinstance(t, int) else pl.multiple_of(t * D, D)

    def weights(t, blocks, held, probs):
        top = jnp.full((8, LANES), NEG, F32)
        for j, (keys, seen) in enumerate(blocks):
            part = jnp.where(seen, dot_nt(keys, qs[t]), NEG)
            held[j * D : (j + 1) * D] = part
            top = jnp.maximum(top, jnp.max(part.reshape(D // 8, 8, LANES), axis=0))
        top = jnp.max(top, axis=0, keepdims=True)
        total = jnp.zeros((8, LANES), F32)
        for j in range(len(blocks)):
            here = slice(j * D, (j + 1) * D)
            part = jnp.exp2(held[here] * LOG2_SCALE - top * LOG2_SCALE)
            probs[here] = part.astype(BF16)
            total = total + jnp.sum(part.reshape(D // 8, 8, LANES), axis=0)
        return top, jnp.sum(total, axis=0, keepdims=True)

    def band_scores(t, _):
        low = jnp.maximum(pos + (BAND + 1) - wide, BAND - (ctx * rows + t * D))
        blocks = [
            (band[0, (t + j) * D : (t + j + 1) * D, :], row_block >= low - j * D) for j in range(BAND // D)
        ]
        blocks.append((band[0, t * D + BAND : (t + 1) * D + BAND, :], row_block <= pos))
        top, total = weights(t, blocks, s_band.at[t % 2], p_band.at[t])
        stat[t, 0:1] = top
        stat[t, 1:2] = total
        return 0

    def band_out(t, _):
        part_t[t] = dot_nn(trans[1, :, pl.ds(at_of(t), KEYS)], p_band[t])
        return 0

    def vert_scores(t, _):
        low = stat[t, 0:1]
        held, probs = s_vert.at[t % 2], p_vert.at[t]
        top = jnp.broadcast_to(low, (8, LANES))
        for j in range(slots):
            here = slice(j * D, (j + 1) * D)
            part = dot_nt(vert[0, here], qs[t]) + hide[t, here]
            held[here] = part
            top = jnp.maximum(top, jnp.max(part.reshape(D // 8, 8, LANES), axis=0))
        top = jnp.max(top, axis=0, keepdims=True)
        total = jnp.zeros((8, LANES), F32)
        for j in range(slots):
            here = slice(j * D, (j + 1) * D)
            part = jnp.exp2(held[here] * LOG2_SCALE - top * LOG2_SCALE)
            probs[here] = part.astype(BF16)
            total = total + jnp.sum(part.reshape(D // 8, 8, LANES), axis=0)
        total = jnp.sum(total, axis=0, keepdims=True)
        less = jnp.exp2((low - top) * LOG2_SCALE)
        inv = 1.0 / (stat[t, 1:2] * less + total)
        stat[t, 2:3] = less * inv
        stat[t, 3:4] = inv
        return 0

    def vert_values(t, _):
        scaled = (gt_band[t].astype(F32) * stat[t, 3:4]).astype(BF16)
        gt_vert[t] = scaled
        gvert[1] += dot_nn(p_vert[t], scaled.T)
        return 0

    def vert_out(t, _):
        of_band, of_vert = stat[t, 2:3], stat[t, 3:4]
        out_t = part_t[t] * of_band + dot_nn(trans[1, :, BAND + rows :], p_vert[t]) * of_vert
        out_t = out_t.astype(BF16)
        ot_sc[t] = out_t
        stat[t, 5:6] = jnp.sum(gt_vert[t].astype(F32) * out_t.astype(F32), axis=0, keepdims=True)
        return 0

    def vert_keys(t, _):
        d_vert = (p_vert[t].astype(F32) * (dot_nn(vert[1], gt_vert[t]) - stat[t, 5:6])).astype(BF16)
        p_vert[t] = d_vert
        gvert[0] += dot_nn(d_vert, qs[t])
        return 0

    def band_values(t, _):
        out_t = ot_sc[t]
        scaled = (gt_band[t].astype(F32) * stat[t, 2:3]).astype(BF16)
        gt_band[t] = scaled
        stat[t, 4:5] = jnp.sum(scaled.astype(F32) * out_t.astype(F32), axis=0, keepdims=True)
        gband[1, pl.ds(at_of(t), KEYS), :] += dot_nn(p_band[t], scaled.T)
        out = out_t.T
        for a in range(GROUP):
            o_sc[t, :, a * D : (a + 1) * D] = out[a * D : (a + 1) * D]
        return 0

    def band_keys(t, _):
        seen = pl.ds(at_of(t), KEYS)
        d_sc[...] = (p_band[t].astype(F32) * (dot_nn(band[1, seen, :], gt_band[t]) - stat[t, 4:5])).astype(BF16)
        dq = dot_nn(trans[0, :, seen], d_sc[...]) + dot_nn(trans[0, :, BAND + rows :], p_vert[t])
        dq = (dq * SCALE).astype(BF16).T
        for a in range(GROUP):
            dq_sc[t, :, a * D : (a + 1) * D] = dq[a * D : (a + 1) * D]
        gband[0, seen, :] += dot_nn(d_sc[...], qs[t])
        return 0

    def run(body, start, stop):
        lax.fori_loop(start, stop, body, 0)

    def scatter(x):
        gvert_out[x] = gvert[x].astype(BF16)
        return to_ctx(
            lambda by: gvert_out.at[x, share(ctx_at(by)), :], lambda by: part2.at[x, by],
            rs2_send.at[x], rs2_recv.at[x], part2.at[x, 1:])

    def give_rim(x):
        rim_out[x] = gband[x, :BAND, :].astype(BF16)
        return to_device(rim_out.at[x], rim_in.at[x, rows - BAND :, :],
                         back_send.at[x], back_recv.at[x], ctx_at(-1), head)

    order = [*range(late, tiles), *range(late)]
    key_terms = have(0)
    for t in range(late, tiles):
        band_scores(t, 0)
    key_rim = lend_rim(0)
    value_terms = have(1)
    run(band_out, late, tiles)
    key_all = spread_sum(
        0, contrib[0, share(ctx), :].astype(F32), part1, key_terms, red1, vert, ag1_send, ag1_recv)
    take_rim(0, key_rim)
    for t in range(late):
        band_scores(t, 0)
    value_all = spread_sum(
        1, contrib[1, share(ctx), :].astype(F32), part1, value_terms, red1, vert, ag1_send, ag1_recv)
    value_rim = lend_rim(1)
    drain(key_all)
    for i in range(tiles + 1):
        if i < tiles:
            vert_scores(order[i], 0)
        if i > 0:
            vert_values(order[i - 1], 0)
    value_terms = scatter(1)
    drain(value_all)
    trans[1, :, BAND + rows :] = vert[1].T

    half = late // 2
    for i in range(tiles + 1):
        if i == tiles - late:
            take_rim(1, value_rim)
        if i < tiles:
            if i >= tiles - late:
                band_out(order[i], 0)
            vert_out(order[i], 0)
        if i > 0:
            vert_keys(order[i - 1], 0)
    key_terms = scatter(0)
    trans[0, :, BAND + rows :] = vert[0].T
    run(band_values, 0, late)
    value_back = give_rim(1)
    value_all = spread_sum(1, gvert[1, share(ctx), :], part2, value_terms, red2, vsum, ag2_send, ag2_recv)
    run(band_values, late, tiles)
    outs = [pltpu.make_async_copy(o_sc, o_hbm, out_sem.at[0])]
    outs[0].start()
    run(band_keys, 0, half)
    key_all = spread_sum(0, gvert[0, share(ctx), :], part2, key_terms, red2, vsum, ag2_send, ag2_recv)
    run(band_keys, half, late)
    key_back = give_rim(0)

    grads = []

    def finish(x, dst, back, everyone):
        back.wait_recv()
        drain(everyone)
        for by in (*head_offsets, 0):
            n = head_at(by)
            total = gband[x, pl.ds(pl.multiple_of(BAND + n * D, D), D), :] + rim_in[x, block(n), :].astype(F32)
            for j in range(slots):
                which = jnp.full((D, D), vertical[0, j], jnp.int32) - first
                total = total + jnp.where(which == n, vsum[x, j * D : (j + 1) * D, :].astype(F32), 0.0)
            if x == 0:
                total = total * SCALE
            final[x, by] = total.astype(BF16)
            if by == 0:
                c = pltpu.make_async_copy(final.at[x, by], dst.at[:, block(head)], grad_local.at[x])
                c.start()
                outs.append(c)
            else:
                to_device(final.at[x, by], dst.at[:, block(head)], grad_send.at[x], grad_recv.at[x], ctx, n)
        unsent.append((final.at[x, 1:], grad_send.at[x]))
        grads.append((final.at[x, 1:], grad_recv.at[x]))

    most = late + (tiles - late) // 2
    run(band_keys, late, most)
    finish(1, dv_hbm, value_back, value_all)
    run(band_keys, most, tiles)
    finish(0, dk_hbm, key_back, key_all)
    outs.append(pltpu.make_async_copy(dq_sc, dq_hbm, out_sem.at[1]))
    outs[-1].start()
    for c in grads + unsent:
        drain(c)
    for c in (key_rim, value_rim, key_back, value_back):
        c.wait_send()
    for c in outs:
        c.wait()


def hand_over(*refs):
    sem = refs[8]
    copies = []
    for i in range(4):
        parts = 4 if i < 2 else 2
        step = refs[i].shape[0] // parts
        for p in range(parts):
            here = pl.ds(p * step, step)
            copies.append(pltpu.make_async_copy(refs[i].at[here], refs[4 + i].at[here], sem.at[len(copies)]))
    for c in copies:
        c.start()
    for c in copies:
        c.wait()


def per_device(ctx_n, head_n, queries, keys, values, grad, vertical, width):
    rows, cols = queries.shape
    tiles = rows // D
    piece = VERT // ctx_n
    any_ = pl.BlockSpec(memory_space=pl.ANY)
    hbm = pl.BlockSpec(memory_space=pltpu.HBM)
    dma = pltpu.SemaphoreType.DMA
    tiled = jax.ShapeDtypeStruct((tiles, D, cols), BF16)
    results = pl.pallas_call(
        functools.partial(kernel, ctx_n, head_n),
        out_shape=(tiled, tiled, jax.ShapeDtypeStruct(keys.shape, BF16), jax.ShapeDtypeStruct(keys.shape, BF16)),
        in_specs=[hbm] * 6,
        out_specs=[any_] * 4,
        scratch_shapes=[
            pltpu.VMEM((tiles, LANES, D), BF16),
            pltpu.VMEM((tiles, LANES, D), BF16),
            pltpu.VMEM((tiles, VERT, LANES), F32),
            pltpu.VMEM((2, *keys.shape), BF16),
            pltpu.VMEM((2, rows, D), BF16),
            pltpu.VMEM((2, BAND + rows, D), BF16),
            pltpu.VMEM((2, D, BAND + rows + VERT), BF16),
            pltpu.VMEM((2, VERT, D), BF16),
            pltpu.VMEM((2, ctx_n, piece, D), BF16),
            pltpu.VMEM((2, piece, D), BF16),
            pltpu.VMEM((2, VERT, D), BF16),
            pltpu.VMEM((2, KEYS, LANES), F32),
            pltpu.VMEM((2, VERT, LANES), F32),
            pltpu.VMEM((tiles, KEYS, LANES), BF16),
            pltpu.VMEM((tiles, VERT, LANES), BF16),
            pltpu.VMEM((KEYS, LANES), BF16),
            pltpu.VMEM((tiles, D, LANES), BF16),
            pltpu.VMEM((tiles, D, LANES), BF16),
            pltpu.VMEM((tiles, 8, LANES), F32),
            pltpu.VMEM((tiles, D, LANES), F32),
            pltpu.VMEM((tiles, D, LANES), BF16),
            pltpu.VMEM((tiles, D, LANES), BF16),
            pltpu.VMEM((tiles, D, LANES), BF16),
            pltpu.VMEM((2, BAND + rows, D), F32),
            pltpu.VMEM((2, VERT, D), F32),
            pltpu.VMEM((2, VERT, D), BF16),
            pltpu.VMEM((2, ctx_n, piece, D), BF16),
            pltpu.VMEM((2, piece, D), BF16),
            pltpu.VMEM((2, VERT, D), BF16),
            pltpu.VMEM((2, BAND, D), BF16),
            pltpu.VMEM((2, rows, D), BF16),
            pltpu.VMEM((2, head_n, D, D), BF16),
            pltpu.SMEM((1, VERT // D), jnp.int32),
            pltpu.SMEM((GROUP,), jnp.int32),
            dma((4,)),
            *[dma((2,))] * 3,
            *[dma((2,))] * 2,
            *[dma((2,))] * 4,
            dma((2,)),
            *[dma((2,))] * 4,
            *[dma((2,))] * 2,
            *[dma((2,))] * 3,
        ],
        compiler_params=pltpu.CompilerParams(
            collective_id=0, has_side_effects=True, vmem_limit_bytes=44 * 1024 * 1024
        ),
        name="vertical_slash",
    )(
        *(
            pltpu.with_memory_space_constraint(x, pltpu.HBM)
            for x in (vertical, width, queries.reshape(tiles, D, cols), keys, values, grad.reshape(tiles, D, cols))
        ),
    )
    o, dq, dk, dv = pl.pallas_call(
        hand_over,
        out_shape=tuple(jax.ShapeDtypeStruct(r.shape, r.dtype) for r in results),
        in_specs=[any_] * 4,
        out_specs=[hbm] * 4,
        scratch_shapes=[dma((12,))],
        compiler_params=pltpu.CompilerParams(vmem_limit_bytes=1024 * 1024),
        name="hand_over",
    )(*results)
    return o.reshape(rows, cols), dq.reshape(rows, cols), dk, dv


def solution(mesh):
    return jax.shard_map(
        functools.partial(per_device, mesh.shape["ctx"], mesh.shape["head"]),
        mesh=mesh,
        in_specs=(
            P("ctx", "head"),
            P(("ctx", "head"), None),
            P(("ctx", "head"), None),
            P("ctx", "head"),
            P("head", None),
            P("head"),
        ),
        out_specs=(
            P("ctx", "head"),
            P("ctx", "head"),
            P(("ctx", "head"), None),
            P(("ctx", "head"), None),
        ),
        check_vma=False,
    )
```
